256 devices in a mesh: gx: 16 (over z, y_lo), gy: 4 (over x), gz: 4 (over y_hi, core).
Axes of the slice: x: 4, y: 4 (y_hi: 2, y_lo: 2; y = y_hi * 2 + y_lo), z: 8, core: 2. Of those that a mesh axis runs over, the one named last changes fastest.
Arguments:
- pressure_start: float32 [256, 256, 1024], P('gx', 'gy', 'gz'), may hold values from -6 to 6
- source: float32 [256, 256, 1024], P('gx', 'gy', 'gz'), may hold values from -16 to 16
- permeability: float32 [256, 256, 1024], P('gx', 'gy', 'gz'), may hold values from 0.1 to 10
Outputs:
- pressure: float32 [256, 256, 1024], P('gx', 'gy', 'gz')
The draws below stay inside these ranges and needn't reach their ends.
All inputs are finite; a program needn't handle non-finite values.
Results may differ from the reference program's by a relative error of at most 0.0003.
Values sent between devices are 32-bit elements; how exact they have to be, the bound alone decides.
A program may use at most 128 MiB of HBM per device.

```python
import math
import jax
import jax.numpy as jnp

RATIO = 8
SWEEPS = 4
COARSE_SWEEPS = 8
NZ = 256
NY = 256
NX = 1024


def draw_source(key, part):
    shape = (NZ, NY, NX)
    cells_z, cells_y, cells_x = (NZ // RATIO, NY // RATIO, NX // RATIO)
    sign_bits = jax.random.randint(jax.random.fold_in(key, 7), (cells_z, cells_y, cells_x), 0, 2)
    signs = sign_bits.astype(jnp.float32) * 2.0 - 1.0
    signs = jnp.broadcast_to(signs[:, None, :, None, :, None], (cells_z, RATIO, cells_y, RATIO, cells_x, RATIO)).reshape(shape)
    depth_pos = jnp.arange(NZ, dtype=jnp.float32).reshape(NZ, 1, 1) / NZ
    smooth = 1.0 + 2.0 * depth_pos
    rough_key = jax.random.fold_in(key, 11)
    rough = 4.0 * jax.random.normal(rough_key, shape, jnp.float32)
    return jnp.clip(12.0 * signs + smooth + rough, -16.0, 16.0)


def level_of(rng, shape, cuts, least, largest):
    def one(axis_at, shards_of):
        draws = jax.random.uniform(jax.random.fold_in(jax.random.fold_in(rng, 6), axis_at), (shards_of,), jnp.float32, least / len(cuts), largest / len(cuts))
        return jnp.repeat(jnp.exp(draws), shape[axis_at] // shards_of).reshape((-1,) + (1,) * (len(shape) - axis_at - 1))

    gain = one(*cuts[0])
    for cut in cuts[1:]:
        gain = gain * one(*cut)
    return gain


def centred(own_key, dims, spread, bound, shards=(), kind=jnp.bfloat16):
    result = jax.random.normal(own_key, dims, jnp.float32) * spread
    if len(shards) > 0:
        result = level_of(own_key, dims, shards, -0.22, 0.18) * result
    return jnp.clip(result, min=-bound, max=bound).astype(kind)


def setup_inputs(seed: int = 0) -> dict:
    seeds = jax.random.split(jax.random.key(seed), 4)
    return {
        "pressure_start": centred(seeds[0], (NZ, NY, NX), 1.0, 6.0, ((0, 16), (1, 4), (2, 4)), jnp.float32),
        "source": draw_source(jax.random.fold_in(seeds[3], 71), 0),
        "permeability": jnp.clip(jnp.exp(math.log(10.0) - 4.6051702 * jax.random.uniform(seeds[2], (NZ, NY, NX), jnp.float32) ** level_of(seeds[2], (NZ, NY, NX), ((0, 16), (1, 4), (2, 4)), -0.2, 0.2)), 0.1, 10.0),
    }


OMEGA = 0.8
OMEGA_COARSE = 0.8


def neighbours(padded):
    return (padded[:-2, 1:-1, 1:-1], padded[2:, 1:-1, 1:-1],
            padded[1:-1, :-2, 1:-1], padded[1:-1, 2:, 1:-1],
            padded[1:-1, 1:-1, :-2], padded[1:-1, 1:-1, 2:])


def face_weights(padded):
    center = padded[1:-1, 1:-1, 1:-1]
    weights = tuple(jnp.where(beside_cell > 0.0, 0.5 * (center + beside_cell), center) for beside_cell in neighbours(padded))
    diagonal_sum = weights[0] + weights[1] + weights[2] + weights[3] + weights[4] + weights[5]
    return weights, diagonal_sum


def apply_operator(padded, weights, diagonal_sum):
    beside = neighbours(padded)
    flux = weights[0] * beside[0] + weights[1] * beside[1] + weights[2] * beside[2]
    flux = flux + weights[3] * beside[3] + weights[4] * beside[4] + weights[5] * beside[5]
    return diagonal_sum * padded[1:-1, 1:-1, 1:-1] - flux


def block_sum(values):
    depth, rows, width = values.shape
    return values.reshape(depth // RATIO, RATIO, rows // RATIO, RATIO, width // RATIO, RATIO).sum(axis=(1, 3, 5))


def coarse_faces(weights):
    depth, rows, width = weights[0].shape
    cells_z, cells_y, cells_x = depth // RATIO, rows // RATIO, width // RATIO
    low_z = weights[0][0::RATIO].reshape(cells_z, cells_y, RATIO, cells_x, RATIO).sum(axis=(2, 4))
    high_z = weights[1][RATIO - 1::RATIO].reshape(cells_z, cells_y, RATIO, cells_x, RATIO).sum(axis=(2, 4))
    low_y = weights[2][:, 0::RATIO, :].reshape(cells_z, RATIO, cells_y, cells_x, RATIO).sum(axis=(1, 4))
    high_y = weights[3][:, RATIO - 1::RATIO, :].reshape(cells_z, RATIO, cells_y, cells_x, RATIO).sum(axis=(1, 4))
    low_x = weights[4][:, :, 0::RATIO].reshape(cells_z, RATIO, cells_y, RATIO, cells_x).sum(axis=(1, 3))
    high_x = weights[5][:, :, RATIO - 1::RATIO].reshape(cells_z, RATIO, cells_y, RATIO, cells_x).sum(axis=(1, 3))
    return (low_z, high_z, low_y, high_y, low_x, high_x)


def prolong_add(fine, correction):
    depth, rows, width = fine.shape
    blocks = fine.reshape(depth // RATIO, RATIO, rows // RATIO, RATIO, width // RATIO, RATIO)
    return (blocks + correction[:, None, :, None, :, None]).reshape(depth, rows, width)


def coarse_sweeps(coarse_rhs, faces, diagonal_sum):
    correction = OMEGA_COARSE * coarse_rhs / diagonal_sum
    for sweep_index in range(COARSE_SWEEPS - 1):
        applied = apply_operator(jnp.pad(correction, 1), faces, diagonal_sum)
        correction = correction + OMEGA_COARSE * (coarse_rhs - applied) / diagonal_sum
    applied = apply_operator(jnp.pad(correction, 1), faces, diagonal_sum)
    leftover = jnp.sum(coarse_rhs - applied)
    shift = leftover / jnp.sum(diagonal_sum)
    return correction + shift


def reference(pressure_start, source, permeability):
    weights, diagonal_sum = face_weights(jnp.pad(permeability, 1))
    applied = apply_operator(jnp.pad(pressure_start, 1), weights, diagonal_sum)
    start_residual = source - applied
    pressure_now = pressure_start + OMEGA * start_residual / diagonal_sum
    for sweep_index in range(SWEEPS - 1):
        applied = apply_operator(jnp.pad(pressure_now, 1), weights, diagonal_sum)
        pressure_now = pressure_now + OMEGA * (source - applied) / diagonal_sum
    faces = coarse_faces(weights)
    coarse_diagonal = faces[0] + faces[1] + faces[2] + faces[3] + faces[4] + faces[5]
    correction = coarse_sweeps(block_sum(start_residual), faces, coarse_diagonal)
    return prolong_add(pressure_now, correction)
```

```python
import jax
import jax.numpy as jnp
from jax import lax
from jax.experimental import pallas as pl
from jax.experimental.pallas import tpu as pltpu
from jax.sharding import PartitionSpec as P

RATIO = 8
SWEEPS = 4
COARSE_SWEEPS = 8
OMEGA = 0.8
MESH = pl.DeviceIdType.MESH

D, R, W = 16, 64, 256
T = R // RATIO
H = W // 2
SLOT = 64
FIRST = 8
CX = W // RATIO
KF = 0


def iota(shape, axis):
    return lax.broadcasted_iota(jnp.int32, shape, axis)


def kernel(
    nx, ny, nz,
    p_hbm, s_hbm, k_hbm, out,
    kx, p0, p1, p2, p3, src, wz, wyl, wyh, wxl, wxh, dia, dinv,
    ysend, yrecv, xsend, xrecv, accs, ebuf, erecv, part1, part2,
    load_sem, fsend, frecv, csend, crecv, a1send, a1recv, a2send, a2recv,
):
    ix, iy, iz = lax.axis_index("gx"), lax.axis_index("gy"), lax.axis_index("gz")
    dirs = (
        ("gx", ix - 1, ix > 0), ("gx", ix + 1, ix < nx - 1),
        ("gy", iy - 1, iy > 0), ("gy", iy + 1, iy < ny - 1),
        ("gz", iz - 1, iz > 0), ("gz", iz + 1, iz < nz - 1),
    )
    press = (p0, p1, p2, p3)
    plane_group = ny * nz
    my_plane = iy * nz + iz

    loads = [
        pltpu.make_async_copy(k_hbm, kx.at[pl.ds(1, D)], load_sem.at[0]),
        pltpu.make_async_copy(p_hbm, p0.at[pl.ds(1, D)], load_sem.at[1]),
        pltpu.make_async_copy(s_hbm, src, load_sem.at[2]),
    ]
    for load in loads:
        load.start()

    barrier = pltpu.get_barrier_semaphore()

    def plane_peer(step):
        other = lax.rem(my_plane + step, plane_group)
        return {"gy": other // nz, "gz": lax.rem(other, nz)}, other

    def line_peer(step):
        other = lax.rem(ix + step, nx)
        return {"gx": other}, other

    for axis, other, exists in dirs:
        @pl.when(exists)
        def _():
            pl.semaphore_signal(barrier, 1, device_id={axis: other}, device_id_type=MESH)

    @pl.loop(1, plane_group)
    def _(step):
        pl.semaphore_signal(barrier, 1, device_id=plane_peer(step)[0], device_id_type=MESH)

    @pl.loop(1, nx)
    def _(step):
        pl.semaphore_signal(barrier, 1, device_id=line_peer(step)[0], device_id_type=MESH)

    near = sum(e.astype(jnp.int32) for _, _, e in dirs)
    lane = iota((1, 128), 1)
    zero_tile = jnp.zeros((8, 128), jnp.float32)

    for d, (_, _, exists) in enumerate(dirs):
        @pl.when(jnp.logical_not(exists))
        def _():
            for f in range(1, 5):
                if d < 2:
                    press[f - 1][d * (D + 1)] = jnp.zeros((R, W), jnp.float32)
                elif d < 4:
                    yrecv[f, d - 2] = jnp.zeros((2, D, H), jnp.float32)
                else:
                    xrecv[f, d - 4] = zero_tile
            for r in range(COARSE_SWEEPS - 1):
                erecv[r, d] = zero_tile

    accs[...] = jnp.zeros(accs.shape, jnp.float32)

    def fine_copy(f, d, incoming=False):
        axis, other, _ = dirs[d]
        end = d ^ 1
        if d < 2:
            field = kx if f == KF else press[f - 1]
            here = field.at[1 if d == 0 else D]
            there = field.at[D + 1 if d == 0 else 0]
            back = field.at[0 if d == 0 else D + 1]
        elif d < 4:
            here, there, back = ysend.at[f, d - 2], yrecv.at[f, end - 2], yrecv.at[f, d - 2]
        else:
            here, there, back = xsend.at[f, d - 4], xrecv.at[f, end - 4], xrecv.at[f, d - 4]
        return pltpu.make_async_remote_copy(
            src_ref=here,
            dst_ref=back if incoming else there,
            send_sem=fsend.at[f, d],
            recv_sem=frecv.at[f, d if incoming else end],
            device_id={axis: other},
            device_id_type=MESH,
        )

    def coarse_copy(r, d, incoming=False):
        axis, other, _ = dirs[d]
        return pltpu.make_async_remote_copy(
            src_ref=ebuf.at[r],
            dst_ref=erecv.at[r, d if incoming else d ^ 1],
            send_sem=csend.at[r, d],
            recv_sem=crecv.at[r, d if incoming else d ^ 1],
            device_id={axis: other},
            device_id_type=MESH,
        )

    def start(make, f, which):
        for d in which:
            @pl.when(dirs[d][2])
            def _():
                make(f, d).start()

    def arrive(make, f, which):
        for d in which:
            @pl.when(dirs[d][2])
            def _():
                make(f, d, True).wait_recv()

    def pack_x(left, right, z, low, high):
        a = zero_tile
        b = zero_tile
        for t in range(T):
            rows = slice(8 * t, 8 * t + 8)
            a = jnp.where(lane == 16 * t, pltpu.roll(left[rows], 16 * t, 1) if t else left[rows], a)
            b = jnp.where(lane == 16 * t, pltpu.roll(right[rows], 16 * t + 1, 1), b)
        a = pltpu.roll(a, z, 1)
        b = pltpu.roll(b, z, 1)
        mine = lax.rem(lane, 16) == z
        return jnp.where(mine, a, low), jnp.where(mine, b, high)

    def unpack_x(f, z):
        back = lax.rem(128 - z, 128)
        low = pltpu.roll(xrecv[f, 0], back, 1)
        high = pltpu.roll(xrecv[f, 1], back, 1)
        lows = [pltpu.roll(low, 128 - 16 * t, 1) if t else low for t in range(T)]
        highs = [pltpu.roll(high, 127 - 16 * t, 1) for t in range(T)]
        return jnp.concatenate(lows, 0), jnp.concatenate(highs, 0)

    row = iota((R, 1), 0)

    def beside(left, right, f, z):
        ylo = [yrecv[f, 0, h, pl.ds(z, 1), :] for h in range(2)]
        yhi = [yrecv[f, 1, h, pl.ds(z, 1), :] for h in range(2)]
        xlo, xhi = unpack_x(f, z)
        low_y = [
            jnp.where(row == 0, g, pltpu.roll(v, 1, 0))
            for v, g in ((left, ylo[0]), (right, ylo[1]))
        ]
        high_y = [
            jnp.where(row == R - 1, g, pltpu.roll(v, R - 1, 0))
            for v, g in ((left, yhi[0]), (right, yhi[1]))
        ]
        rl, rr = pltpu.roll(left, 1, 1), pltpu.roll(right, 1, 1)
        low_x = [jnp.where(lane == 0, xlo, rl), jnp.where(lane == 0, rl, rr)]
        sl, sr = pltpu.roll(left, H - 1, 1), pltpu.roll(right, H - 1, 1)
        high_x = [jnp.where(lane == H - 1, sr, sl), jnp.where(lane == H - 1, xhi, sr)]
        return low_y, high_y, low_x, high_x

    def keep_faces(f, z, halves, low, high):
        for h, v in enumerate(halves):
            ysend[f, 0, h, pl.ds(z, 1), :] = v[0:1]
            ysend[f, 1, h, pl.ds(z, 1), :] = v[R - 1 : R]
        return pack_x(halves[0], halves[1], z, low, high)

    def keep_packed(f, low, high):
        xsend[f, 0] = low
        xsend[f, 1] = high

    loads[0].wait()
    loads[1].wait()
    pl.semaphore_wait(barrier, near + (plane_group - 1) + (nx - 1))
    start(fine_copy, KF, (0, 1))

    for f, field in ((KF, kx), (1, p0)):
        def pack(z, faces, field=field, f=f):
            return keep_faces(f, z, (field[z + 1, :, :H], field[z + 1, :, H:]), *faces)

        keep_packed(f, *lax.fori_loop(0, D, pack, (zero_tile, zero_tile)))
        start(fine_copy, f, (2, 3, 4, 5))
        if f == KF:
            start(fine_copy, 1, (0, 1))

    for d, (_, _, exists) in enumerate(dirs):
        @pl.when(jnp.logical_not(exists))
        def _():
            if d < 2:
                kx[d * (D + 1)] = kx[1 + d * (D - 1)]
            elif d < 4:
                yrecv[KF, d - 2] = ysend[KF, d - 2]
            else:
                xrecv[KF, d - 4] = xsend[KF, d - 4]

    arrive(fine_copy, KF, range(6))

    def weigh(z, carry):
        halves = (kx[z + 1, :, :H], kx[z + 1, :, H:])
        around = beside(halves[0], halves[1], KF, z)
        c = z // RATIO
        for h in range(2):
            cols = slice(h * H, (h + 1) * H)
            k = halves[h]
            low_z = 0.5 * (k + kx[z, :, cols])
            high_z = 0.5 * (k + kx[z + 2, :, cols])
            faces = [0.5 * (k + g[h]) for g in around]
            wz[z, :, cols] = low_z
            total = low_z + high_z + faces[0] + faces[1] + faces[2] + faces[3]
            for n, (ref, face) in enumerate(zip((wyl, wyh, wxl, wxh), faces)):
                ref[z, :, cols] = face
                accs[1 + n, c, :, cols] += face
            dia[z, :, cols] = total
            dinv[z, :, cols] = OMEGA / total
        return carry

    lax.fori_loop(0, D, weigh, 0)
    wz[D] = 0.5 * (kx[D] + kx[D + 1])
    loads[2].wait()

    def sweep_plane(n, z, faces):
        v_ref = press[n - 1]
        halves = (v_ref[z + 1, :, :H], v_ref[z + 1, :, H:])
        around = beside(halves[0], halves[1], n, z)
        new = []
        for h in range(2):
            cols = slice(h * H, (h + 1) * H)
            v = halves[h]
            flux = wz[z, :, cols] * v_ref[z, :, cols] + wz[z + 1, :, cols] * v_ref[z + 2, :, cols]
            for ref, g in zip((wyl, wyh, wxl, wxh), around):
                flux = flux + ref[z, :, cols] * g[h]
            flux = src[z, :, cols] + flux
            if n == 1:
                accs[0, z // RATIO, :, cols] += flux - dia[z, :, cols] * v
            v = (1.0 - OMEGA) * v + dinv[z, :, cols] * flux
            if n < SWEEPS:
                press[n][z + 1, :, cols] = v
            else:
                out[z, :, cols] = v
            new.append(v)
        if n == SWEEPS:
            return faces
        return keep_faces(n + 1, z, new, *faces)

    def sweep(n):
        arrive(fine_copy, n, range(6))
        faces = (zero_tile, zero_tile)
        faces = lax.fori_loop(
            0, 2, lambda i, fc: sweep_plane(n, i * (D - 1), fc), faces
        )
        faces = lax.fori_loop(1, 3, lambda z, fc: sweep_plane(n, z, fc), faces)
        if n < SWEEPS:
            start(fine_copy, n + 1, (0, 1))
        faces = lax.fori_loop(3, D - 1, lambda z, fc: sweep_plane(n, z, fc), faces)
        if n < SWEEPS:
            keep_packed(n + 1, *faces)
            start(fine_copy, n + 1, (2, 3, 4, 5))

    sweep(1)

    column, spot = iota((W, 128), 0), iota((W, 128), 1)

    def pick(c, offset):
        hit = spot == c * SLOT + FIRST + column // RATIO
        if offset is not None:
            hit = jnp.logical_and(hit, lax.rem(column, RATIO) == offset)
        return jnp.where(hit, 1.0, 0.0).astype(jnp.float32)

    def dot(a, b):
        return jnp.dot(a, b, precision=lax.Precision.HIGHEST, preferred_element_type=jnp.float32)

    def tile_sum(plane):
        return jnp.sum(plane.reshape(T, RATIO, W), axis=1)

    totals = None
    for c in range(2):
        summed = jnp.concatenate(
            [
                tile_sum(accs[0, c]),
                tile_sum(wz[RATIO * c]),
                tile_sum(wz[RATIO * c + RATIO]),
                accs[1, c].reshape(T, RATIO, W)[:, 0],
                accs[2, c].reshape(T, RATIO, W)[:, RATIO - 1],
            ],
            axis=0,
        )
        parts = [
            dot(summed, pick(c, None)),
            dot(tile_sum(accs[3, c]), pick(c, 0)),
            dot(tile_sum(accs[4, c]), pick(c, RATIO - 1)),
        ]
        both = jnp.concatenate(parts, axis=0)
        totals = both if totals is None else totals + both
    rhs, zl, zh, yl, yh, xl, xh = [totals[8 * n : 8 * n + 8] for n in range(7)]
    cdiag = zl + zh + yl + yh + xl + xh
    inside = lax.rem(lane, SLOT)
    valid = jnp.logical_and(inside >= FIRST, inside < FIRST + CX)
    scale = jnp.where(valid, OMEGA / jnp.where(valid, cdiag, 1.0), 0.0)
    fixed = scale * rhs
    sides = [scale * w for w in (zl, zh, yl, yh, xl, xh)]

    tile_row = iota((8, 1), 0)
    even = lane < SLOT
    edges = (
        even, jnp.logical_not(even), tile_row == 0, tile_row == 7,
        inside == FIRST, inside == FIRST + CX - 1,
    )

    def coarse_sweep(r):
        e = ebuf[r]
        arrive(coarse_copy, r, range(6))
        other_plane = pltpu.roll(e, SLOT, 1)
        around = (
            jnp.where(edges[0], pltpu.roll(erecv[r, 0], SLOT, 1), other_plane),
            jnp.where(edges[1], pltpu.roll(erecv[r, 1], SLOT, 1), other_plane),
            jnp.where(edges[2], pltpu.roll(erecv[r, 2], 1, 0), pltpu.roll(e, 1, 0)),
            jnp.where(edges[3], pltpu.roll(erecv[r, 3], 7, 0), pltpu.roll(e, 7, 0)),
            jnp.where(edges[4], pltpu.roll(erecv[r, 4], 128 - (CX - 1), 1), pltpu.roll(e, 1, 1)),
            jnp.where(edges[5], pltpu.roll(erecv[r, 5], CX - 1, 1), pltpu.roll(e, 127, 1)),
        )
        e = (1.0 - OMEGA) * e + fixed
        for w, g in zip(sides, around):
            e = e + w * g
        return e

    def publish(r, e):
        ebuf[r] = e
        if r < COARSE_SWEEPS - 1:
            start(coarse_copy, r, range(6))

    publish(0, fixed)
    for r in range(COARSE_SWEEPS - 1):
        publish(r + 1, coarse_sweep(r))
        if r in (1, 3, 5):
            sweep(2 + r // 2)
    swept = ebuf[COARSE_SWEEPS - 1]

    outside = zero_tile
    for (_, _, exists), edge, w in zip(dirs, edges, (zl, zh, yl, yh, xl, xh)):
        gone = jnp.where(exists, 0.0, 1.0)
        outside = outside + jnp.where(edge, gone * w, 0.0)

    def share(buf, ssem, rsem, count, me, peer_of):
        @pl.loop(1, count)
        def _(step):
            peer, other = peer_of(step)
            pltpu.make_async_remote_copy(
                src_ref=buf.at[me], dst_ref=buf.at[me], send_sem=ssem.at[other],
                recv_sem=rsem.at[me], device_id=peer, device_id_type=MESH,
            ).start()

        def finish():
            @pl.loop(1, count)
            def _(step):
                peer, other = peer_of(step)
                pltpu.make_async_remote_copy(
                    src_ref=buf.at[me], dst_ref=buf.at[other], send_sem=ssem.at[other],
                    recv_sem=rsem.at[other], device_id=peer, device_id_type=MESH,
                ).wait_recv()
            return jnp.sum(buf[...], axis=0)

        def drain():
            @pl.loop(1, count)
            def _(step):
                peer, other = peer_of(step)
                pltpu.make_async_remote_copy(
                    src_ref=buf.at[me], dst_ref=buf.at[me], send_sem=ssem.at[other],
                    recv_sem=rsem.at[me], device_id=peer, device_id_type=MESH,
                ).wait_send()

        return finish, drain

    part1[my_plane, 0] = rhs - outside * swept
    part1[my_plane, 1] = cdiag
    finish1, drain1 = share(part1, a1send, a1recv, plane_group, my_plane, plane_peer)

    spread = [
        lax.dot_general(
            swept, pick(c, None), (((1,), (1,)), ((), ())),
            precision=lax.Precision.HIGHEST, preferred_element_type=jnp.float32,
        )
        for c in range(2)
    ]
    for c in range(2):
        wide = jnp.broadcast_to(spread[c][:, None, :], (T, RATIO, W)).reshape(R, W)
        accs[0, c] = wide

    part2[ix] = finish1()
    finish2, drain2 = share(part2, a2send, a2recv, nx, ix, line_peer)

    def add_spread(z, carry):
        out[z] = out[z] + accs[0, z // RATIO]
        return carry

    lax.fori_loop(0, D, add_spread, 0)

    for f in range(5):
        for d in range(6):
            @pl.when(dirs[d][2])
            def _():
                fine_copy(f, d).wait_send()
    for r in range(COARSE_SWEEPS - 1):
        for d in range(6):
            @pl.when(dirs[d][2])
            def _():
                coarse_copy(r, d).wait_send()
    drain1()

    sums = finish2()
    drain2()
    shift = jnp.sum(sums[0]) / jnp.sum(sums[1])

    def add_shift(z, carry):
        out[z] = out[z] + shift
        return carry

    lax.fori_loop(0, D, add_shift, 0)


def solution(mesh):
    nx, ny, nz = mesh.shape["gx"], mesh.shape["gy"], mesh.shape["gz"]
    f32 = jnp.float32
    dma = pltpu.SemaphoreType.DMA
    rounds = COARSE_SWEEPS - 1

    def body(*refs):
        kernel(nx, ny, nz, *refs)

    def shards(pressure_start, source, permeability):
        block = pltpu.VMEM((D, R, W), f32)
        wide = pltpu.VMEM((D + 2, R, W), f32)
        return pl.pallas_call(
            body,
            out_shape=jax.ShapeDtypeStruct((D, R, W), f32),
            in_specs=[pl.BlockSpec(memory_space=pl.ANY)] * 3,
            out_specs=pl.BlockSpec(memory_space=pltpu.VMEM),
            scratch_shapes=[
                wide, wide, wide, wide, wide,
                block, pltpu.VMEM((D + 1, R, W), f32), block, block, block, block, block, block,
                pltpu.VMEM((5, 2, 2, D, H), f32), pltpu.VMEM((5, 2, 2, D, H), f32),
                pltpu.VMEM((5, 2, 8, 128), f32), pltpu.VMEM((5, 2, 8, 128), f32),
                pltpu.VMEM((5, 2, R, W), f32),
                pltpu.VMEM((COARSE_SWEEPS, 8, 128), f32), pltpu.VMEM((rounds, 6, 8, 128), f32),
                pltpu.VMEM((ny * nz, 2, 8, 128), f32), pltpu.VMEM((nx, 2, 8, 128), f32),
                dma((3,)), dma((5, 6)), dma((5, 6)), dma((rounds, 6)), dma((rounds, 6)),
                dma((ny * nz,)), dma((ny * nz,)), dma((nx,)), dma((nx,)),
            ],
            compiler_params=pltpu.CompilerParams(
                collective_id=0, has_side_effects=True, vmem_limit_bytes=40 << 20
            ),
        )(pressure_start, source, permeability)

    spec = P("gx", "gy", "gz")
    return jax.shard_map(
        shards, mesh=mesh, in_specs=(spec, spec, spec), out_specs=spec, check_vma=False
    )
```

```python
import jax
import jax.numpy as jnp
from jax import lax
from jax.experimental import pallas as pl
from jax.experimental.pallas import tpu as pltpu
from jax.sharding import PartitionSpec as P

RATIO = 8
SWEEPS = 4
COARSE_SWEEPS = 8
OMEGA = 0.8
MESH = pl.DeviceIdType.MESH

D, R, W = 16, 64, 256
T = R // RATIO
H = W // 2
TOP = 8
SLOT = 64
FIRST = 8
CX = W // RATIO
REACH = 4
BLOCKS = 2 * REACH + 1
KF = 0
GROUP = 16


def iota(shape, axis):
    return lax.broadcasted_iota(jnp.int32, shape, axis)


def split3(a):
    high = a.astype(jnp.bfloat16)
    rest = a - high.astype(jnp.float32)
    mid = rest.astype(jnp.bfloat16)
    low = (rest - mid.astype(jnp.float32)).astype(jnp.bfloat16)
    return jnp.concatenate([high, mid, low], axis=0)


def select_dot(a, matrix, contract):
    n = a.shape[0]
    b = lax.dot_general(
        split3(a), matrix, (((1,), (contract,)), ((), ())), preferred_element_type=jnp.float32
    )
    return b[:n] + b[n : 2 * n] + b[2 * n :]


def kernel(
    nx, ny, nz,
    p_hbm, s_hbm, k_hbm, out, shift_out,
    kx, p0, p1, p2, p3, src, wz, wyl, wyh, wxl, wxh, dia, dinv, acc, gsum, gpick, corr,
    xsend, xrecv, own_w, xw, zw, yw, own_f, xf, zf, yf, sides, part1, part2,
    load_sem, fsend, frecv, cxs, cxr, czs, czr, cys, cyr, a1send, a1recv, a2send, a2recv,
):
    ix, iy, iz = lax.axis_index("gx"), lax.axis_index("gy"), lax.axis_index("gz")
    dirs = (
        ("gx", ix - 1, ix > 0), ("gx", ix + 1, ix < nx - 1),
        ("gy", iy - 1, iy > 0), ("gy", iy + 1, iy < ny - 1),
        ("gz", iz - 1, iz > 0), ("gz", iz + 1, iz < nz - 1),
    )
    press = (p0, p1, p2, p3)
    plane_group = ny * nz
    my_plane = iy * nz + iz
    own = pl.ds(TOP, R)
    planes = pl.ds(1, D)

    loads = []
    for n, (ref, place) in enumerate(((k_hbm, kx), (p_hbm, p0), (s_hbm, src))):
        for h in range(2):
            there = place.at[h, planes, own] if n < 2 else place.at[h]
            loads.append(
                pltpu.make_async_copy(ref.at[:, :, pl.ds(h * H, H)], there, load_sem.at[n, h])
            )
    for load in loads:
        load.start()

    barrier = pltpu.get_barrier_semaphore()

    def plane_peer(step):
        other = lax.rem(my_plane + step, plane_group)
        return {"gy": other // nz, "gz": lax.rem(other, nz)}, other

    def line_peer(step):
        other = lax.rem(ix + step, nx)
        return {"gx": other}, other

    for axis, other, exists in dirs:
        @pl.when(exists)
        def _():
            pl.semaphore_signal(barrier, 1, device_id={axis: other}, device_id_type=MESH)

    @pl.loop(1, plane_group)
    def _(step):
        pl.semaphore_signal(barrier, 1, device_id=plane_peer(step)[0], device_id_type=MESH)

    @pl.loop(1, nx)
    def _(step):
        pl.semaphore_signal(barrier, 1, device_id=line_peer(step)[0], device_id_type=MESH)

    near = sum(e.astype(jnp.int32) for _, _, e in dirs)
    lane = iota((1, 128), 1)
    zero_tile = jnp.zeros((8, 128), jnp.float32)
    edge_row = (TOP, TOP + R - 1)
    ghost_row = (TOP - 1, TOP + R)

    for d, (_, _, exists) in enumerate(dirs):
        @pl.when(jnp.logical_not(exists))
        def _():
            for f in range(1, 5):
                if d < 2:
                    press[f - 1][:, d * (D + 1), own] = jnp.zeros((2, R, H), jnp.float32)
                elif d < 4:
                    row = pl.ds(ghost_row[d - 2], 1)
                    press[f - 1][:, planes, row] = jnp.zeros((2, D, 1, H), jnp.float32)
                else:
                    xrecv[f, d - 4] = zero_tile
            if d >= 4:
                for place in (xw, xf):
                    place[d - 4] = jnp.zeros(place.shape[1:], jnp.float32)
            elif d >= 2:
                for place in (yw, yf):
                    place[d - 2] = jnp.zeros(place.shape[1:], jnp.float32)
    far = {}
    for dz in range(-REACH, REACH + 1):
        if dz:
            far[dz] = jnp.logical_and(ix + dz >= 0, ix + dz < nx)

            @pl.when(jnp.logical_not(far[dz]))
            def _():
                for place in (zw, zf):
                    place[dz + REACH] = jnp.zeros(place.shape[1:], jnp.float32)

    acc[...] = jnp.zeros(acc.shape, jnp.float32)

    def fine_copy(f, d, incoming=False):
        axis, other, _ = dirs[d]
        end = d ^ 1
        field = kx if f == KF else press[f - 1]
        if d < 2:
            here = field.at[:, 1 if d == 0 else D, own]
            there = field.at[:, D + 1 if d == 0 else 0, own]
            back = field.at[:, 0 if d == 0 else D + 1, own]
        elif d < 4:
            here = field.at[:, planes, pl.ds(edge_row[d - 2], 1)]
            there = field.at[:, planes, pl.ds(ghost_row[end - 2], 1)]
            back = field.at[:, planes, pl.ds(ghost_row[d - 2], 1)]
        else:
            here, there, back = xsend.at[f, d - 4], xrecv.at[f, end - 4], xrecv.at[f, d - 4]
        return pltpu.make_async_remote_copy(
            src_ref=here,
            dst_ref=back if incoming else there,
            send_sem=fsend.at[f, d],
            recv_sem=frecv.at[f, d if incoming else end],
            device_id={axis: other},
            device_id_type=MESH,
        )

    groups = ((own_w, xw, zw, yw), (own_f, xf, zf, yf))

    def coarse_copy(q, stage, way, incoming=False):
        own_q, x_q, z_q, y_q = groups[q]
        if stage == "z":
            here, place = z_q.at[REACH], z_q
            slot = REACH + way if incoming else REACH - way
            sems, to = (czs, czr), {"gx": ix + way}
            sent = REACH + way
        else:
            axis, other, _ = dirs[(4 if stage == "x" else 2) + way]
            here, place = (own_q, x_q) if stage == "x" else (z_q.at[pl.ds(1, BLOCKS - 2)], y_q)
            slot = way if incoming else 1 - way
            sems, to = (cxs, cxr) if stage == "x" else (cys, cyr), {axis: other}
            sent = way
        return pltpu.make_async_remote_copy(
            src_ref=here, dst_ref=place.at[slot], send_sem=sems[0].at[q, sent],
            recv_sem=sems[1].at[q, slot], device_id=to, device_id_type=MESH,
        )

    def ways(stage):
        if stage == "z":
            return list(far.items())
        first = 4 if stage == "x" else 2
        return [(way, dirs[first + way][2]) for way in range(2)]

    def coarse_start(q, stage):
        for way, exists in ways(stage):
            @pl.when(exists)
            def _():
                coarse_copy(q, stage, way).start()

    def coarse_arrive(q, stage):
        for way, exists in ways(stage):
            @pl.when(exists)
            def _():
                coarse_copy(q, stage, way, True).wait_recv()

    def coarse_sent(q, stage):
        for way, exists in ways(stage):
            @pl.when(exists)
            def _():
                coarse_copy(q, stage, way).wait_send()

    def start(make, f, which):
        for d in which:
            @pl.when(dirs[d][2])
            def _():
                make(f, d).start()

    def arrive(make, f, which):
        for d in which:
            @pl.when(dirs[d][2])
            def _():
                make(f, d, True).wait_recv()

    def edges_of(columns, offsets):
        low, high = zero_tile, zero_tile
        for j, at in enumerate(offsets):
            for t in range(T):
                to = 16 * t + at
                left = columns(j, 0, t)
                low = jnp.where(lane == to, pltpu.roll(left, to, 1) if to else left, low)
                right = columns(j, 1, t)
                high = jnp.where(lane == to, pltpu.roll(right, (to + 1) % 128, 1), high)
        return low, high

    def keep_packed(f, faces):
        xsend[f, 0] = faces[0]
        xsend[f, 1] = faces[1]

    def ghosts(f, base, offsets):
        low = pltpu.roll(xrecv[f, 0], lax.rem(128 - base, 128), 1)
        high = pltpu.roll(xrecv[f, 1], lax.rem(128 - base, 128), 1)
        lows, highs = [], []
        for at in offsets:
            lows.append([pltpu.roll(low, (128 - 16 * t - at) % 128, 1) for t in range(T)])
            highs.append([pltpu.roll(high, (255 - 16 * t - at) % 128, 1) for t in range(T)])
        return lows, highs

    def around(field, z, g, low_ghosts, high_ghosts):
        n = GROUP // 8
        lows = jnp.concatenate(low_ghosts[g * n : g * n + n], 0)
        highs = jnp.concatenate(high_ghosts[g * n : g * n + n], 0)
        at = TOP + g * GROUP
        own_rows = [field[h, z + 1, pl.ds(at, GROUP), :] for h in range(2)]
        low_y = [field[h, z + 1, pl.ds(at - 1, GROUP), :] for h in range(2)]
        high_y = [field[h, z + 1, pl.ds(at + 1, GROUP), :] for h in range(2)]
        rl, rr = [pltpu.roll(v, 1, 1) for v in own_rows]
        low_x = [jnp.where(lane == 0, lows, rl), jnp.where(lane == 0, rl, rr)]
        sl, sr = [pltpu.roll(v, H - 1, 1) for v in own_rows]
        high_x = [jnp.where(lane == H - 1, sr, sl), jnp.where(lane == H - 1, highs, sr)]
        return own_rows, low_y, high_y, low_x, high_x

    loads[0].wait()
    loads[1].wait()
    loads[2].wait()
    loads[3].wait()

    def pack(i, faces):
        z = 4 * i
        mine = lax.rem(lane, 16) // 4 == i
        result = []
        for n, field in enumerate((kx, p0)):
            fresh = edges_of(
                lambda j, h, t: field[h, z + 1 + j, pl.ds(TOP + 8 * t, 8), :], range(4)
            )
            for m in range(2):
                moved = pltpu.roll(fresh[m], z, 1)
                result.append(jnp.where(mine, moved, faces[2 * n + m]))
        return tuple(result)

    packed = lax.fori_loop(0, D // 4, pack, (zero_tile,) * 4)
    keep_packed(KF, packed[:2])
    keep_packed(1, packed[2:])

    for d, (_, _, exists) in enumerate(dirs):
        @pl.when(jnp.logical_not(exists))
        def _():
            if d < 2:
                kx[:, d * (D + 1), own] = kx[:, 1 + d * (D - 1), own]
            elif d < 4:
                kx[:, planes, pl.ds(ghost_row[d - 2], 1)] = kx[:, planes, pl.ds(edge_row[d - 2], 1)]
            else:
                xrecv[KF, d - 4] = xsend[KF, d - 4]

    pl.semaphore_wait(barrier, near + (plane_group - 1) + (nx - 1))
    start(fine_copy, KF, (4, 5, 2, 3, 0, 1))
    start(fine_copy, 1, (4, 5, 2, 3, 0, 1))

    column, spot = iota((W, 128), 0), iota((W, 128), 1)
    home = spot == FIRST + column // RATIO
    gsum[...] = jnp.where(home, 1.0, 0.0).astype(jnp.bfloat16)
    gpick[...] = jnp.where(
        jnp.logical_and(home, lax.rem(column, RATIO) == 0), 1.0, 0.0
    ).astype(jnp.bfloat16)

    arrive(fine_copy, KF, range(6))

    def weigh(i, carry):
        zs = (2 * i, 2 * i + 1)
        lows, highs = ghosts(KF, zs[0], (0, 1))
        for j, z in enumerate(zs):
            for g in range(R // GROUP):
                rows = pl.ds(g * GROUP, GROUP)
                k, *others = around(kx, z, g, lows[j], highs[j])
                for h in range(2):
                    at = pl.ds(TOP + g * GROUP, GROUP)
                    half = 0.5 * k[h]
                    low_z = half + 0.5 * kx[h, z, at, :]
                    high_z = half + 0.5 * kx[h, z + 2, at, :]
                    total = low_z + high_z
                    wz[h, z, rows, :] = low_z
                    for ref, other in zip((wyl, wyh, wxl, wxh), others):
                        face = half + 0.5 * other[h]
                        ref[h, z, rows, :] = face
                        total = total + face
                    dia[h, z, rows, :] = total
                    dinv[h, z, rows, :] = OMEGA / total
        return carry

    lax.fori_loop(0, D // 2, weigh, 0)
    for h in range(2):
        wz[h, D] = 0.5 * (kx[h, D, own, :] + kx[h, D + 1, own, :])

    def tile_sum(plane):
        return jnp.sum(plane.reshape(T, RATIO, H), axis=1)

    def wide(parts):
        return jnp.concatenate(parts, axis=1)

    def halves(make):
        return wide([make(0), make(1)])

    def sum_planes(c, load):
        total = load(RATIO * c)
        for z in range(RATIO * c + 1, RATIO * c + RATIO):
            total = total + load(z)
        return total

    def every(ref, h, c, first):
        return sum_planes(c, lambda z: ref[h, z, pl.ds(first, T, stride=RATIO), :])

    summed, picked, last = [], [], []
    for c in range(2):
        summed += [
            halves(lambda h: tile_sum(wz[h, RATIO * c])),
            halves(lambda h: tile_sum(wz[h, RATIO * c + RATIO])),
            halves(lambda h: every(wyl, h, c, 0)),
            halves(lambda h: every(wyh, h, c, RATIO - 1)),
        ]
        picked.append(halves(lambda h: tile_sum(sum_planes(c, lambda z: wxl[h, z]))))
        last.append(tile_sum(sum_planes(c, lambda z: wxh[1, z])))
    sums = select_dot(jnp.concatenate(summed, 0), gsum[...], 0)
    picks = select_dot(jnp.concatenate(picked, 0), gpick[...], 0)

    def pair(low, high):
        return low + pltpu.roll(high, SLOT, 1)

    zl, zh, yl, yh = [pair(sums[8 * n : 8 * n + 8], sums[8 * n + 32 : 8 * n + 40]) for n in range(4)]
    xl = pair(picks[:8], picks[8:])
    inside = lax.rem(lane, SLOT)
    final_lane = FIRST + CX - 1
    xh = pltpu.roll(xl, 127, 1)
    for c in range(2):
        to = c * SLOT + final_lane
        xh = jnp.where(lane == to, pltpu.roll(last[c], (to + 1) % 128, 1), xh)
    valid = jnp.logical_and(inside >= FIRST, inside <= final_lane)
    xh = jnp.where(valid, xh, 0.0)
    cdiag = zl + zh + yl + yh + xl + xh
    scale = jnp.where(valid, OMEGA / jnp.where(valid, cdiag, 1.0), 0.0)
    weights = (zl, zh, yl, yh, xl, xh)
    for n, field in enumerate((zl, yl, xl, scale)):
        own_w[n] = field
    coarse_start(0, "x")
    tile_row = iota((8, 1), 0)
    even = lane < SLOT
    edges = (
        even, jnp.logical_not(even), tile_row == 0, tile_row == 7,
        inside == FIRST, inside == final_lane,
    )
    outside = zero_tile
    for (_, _, exists), edge, w in zip(dirs, edges, weights):
        gone = jnp.where(exists, 0.0, 1.0)
        outside = outside + jnp.where(edge, gone * w, 0.0)
    diag_sum = jnp.sum(cdiag, keepdims=True)

    loads[4].wait()
    loads[5].wait()

    def sweep_planes(n, base, offsets, faces, placed=None):
        field = press[n - 1]
        lows, highs = ghosts(n, base, offsets)
        tiles = {}
        for j, at_z in enumerate(offsets):
            z = base + at_z
            for g in range(R // GROUP):
                rows = pl.ds(g * GROUP, GROUP)
                v, *others = around(field, z, g, lows[j], highs[j])
                for h in range(2):
                    at = pl.ds(TOP + g * GROUP, GROUP)
                    flux = src[h, z, rows, :] + wz[h, z, rows, :] * field[h, z, at, :]
                    flux = flux + wz[h, z + 1, rows, :] * field[h, z + 2, at, :]
                    for ref, other in zip((wyl, wyh, wxl, wxh), others):
                        flux = flux + ref[h, z, rows, :] * other[h]
                    if n == 1:
                        acc[h, z // RATIO, rows, :] += flux - dia[h, z, rows, :] * v[h]
                    new = (1.0 - OMEGA) * v[h] + dinv[h, z, rows, :] * flux
                    if n < SWEEPS:
                        press[n][h, z + 1, at, :] = new
                        for t in range(GROUP // 8):
                            tiles[j, h, g * (GROUP // 8) + t] = new[8 * t : 8 * t + 8]
                    else:
                        out[z, rows, pl.ds(h * H, H)] = new + corr[z // RATIO, h, rows, :]
        if n == SWEEPS:
            return faces
        fresh = edges_of(lambda j, h, t: tiles[j, h, t], offsets)
        if placed is None:
            return fresh
        place = lax.rem(lane, 16)
        mine = jnp.logical_and(place >= base + offsets[0], place <= base + offsets[-1])
        return tuple(jnp.where(mine, pltpu.roll(a, base, 1), b) for a, b in zip(fresh, faces))

    def sweep(n):
        arrive(fine_copy, n, range(6))
        if n == SWEEPS:
            lax.fori_loop(0, D // 2, lambda i, c: sweep_planes(n, 2 * i, (0, 1), c, True), 0)
            return
        faces = sweep_planes(n, 0, (0, D - 1), None)

        def inner(i, faces):
            return sweep_planes(n, 2 * i + 1, (0, 1), faces, True)

        faces = lax.fori_loop(0, 1, inner, faces)
        start(fine_copy, n + 1, (0, 1))
        faces = lax.fori_loop(1, D // 2 - 1, inner, faces)
        keep_packed(n + 1, faces)
        start(fine_copy, n + 1, (4, 5, 2, 3))

    sweep(1)

    resid = select_dot(
        jnp.concatenate([halves(lambda h: tile_sum(acc[h, c])) for c in range(2)], 0), gsum[...], 0
    )
    rhs = pair(resid[:8], resid[8:])
    fixed = scale * rhs

    own_f[0] = fixed
    coarse_start(1, "x")

    def merge(q):
        own_q, x_q, z_q, _ = groups[q]
        for n in range(own_q.shape[0]):
            low, high = pltpu.roll(x_q[0, n], 128 - CX, 1), pltpu.roll(x_q[1, n], CX, 1)
            after = jnp.logical_and(inside > final_lane, inside <= final_lane + RATIO)
            z_q[REACH, n] = jnp.where(inside < FIRST, low, jnp.where(after, high, own_q[n]))

    for stage, later in (("x", "z"), ("z", "y")):
        for q in range(2):
            coarse_arrive(q, stage)
            if stage == "x":
                merge(q)
            coarse_start(q, later)

    sweep(2)

    def extended(q, b, n):
        _, _, z_q, y_q = groups[q]
        if b in (0, BLOCKS - 1):
            return jnp.concatenate([zero_tile, z_q[b, n], zero_tile], 0)
        return jnp.concatenate([y_q[0, b - 1, n], z_q[b, n], y_q[1, b - 1, n]], 0)

    def other_slot(v):
        return pltpu.roll(v, SLOT, 1)

    coarse_arrive(0, "y")
    turned = [other_slot(extended(0, b, 0)) for b in range(BLOCKS)]
    tall = 3 * RATIO
    for b in range(1, BLOCKS - 1):
        wz_b, wy_b, wx_b, scale_b = [extended(0, b, n) for n in range(4)]
        high = (
            jnp.where(even, turned[b], turned[b + 1]),
            pltpu.roll(wy_b, tall - 1, 0),
            pltpu.roll(wx_b, 127, 1),
        )
        for n, w in enumerate((wz_b, high[0], wy_b, high[1], wx_b, high[2])):
            sides[b - 1, n] = scale_b * w

    coarse_arrive(1, "y")
    start_values = [extended(1, b, 0) for b in range(BLOCKS)]
    e = list(start_values)
    for m in range(1, COARSE_SWEEPS):
        turned = [other_slot(v) for v in e]
        following = list(e)
        for b in range(1, BLOCKS - 1):
            if 2 * abs(b - REACH) - 1 > COARSE_SWEEPS - 1 - m:
                continue
            beside = (
                jnp.where(even, turned[b - 1], turned[b]),
                jnp.where(even, turned[b], turned[b + 1]),
                pltpu.roll(e[b], 1, 0),
                pltpu.roll(e[b], tall - 1, 0),
                pltpu.roll(e[b], 1, 1),
                pltpu.roll(e[b], 127, 1),
            )
            new = (1.0 - OMEGA) * e[b] + start_values[b]
            for n, g in enumerate(beside):
                new = new + sides[b - 1, n] * g
            following[b] = new
        e = following
    swept = e[REACH][RATIO : 2 * RATIO]

    def share(buf, ssem, rsem, count, me, peer_of):
        def copy(step, incoming):
            peer, other = peer_of(step)
            return pltpu.make_async_remote_copy(
                src_ref=buf.at[me], dst_ref=buf.at[other if incoming else me],
                send_sem=ssem.at[other], recv_sem=rsem.at[other if incoming else me],
                device_id=peer, device_id_type=MESH,
            )

        @pl.loop(1, count)
        def _(step):
            copy(step, False).start()

        def finish():
            @pl.loop(1, count)
            def _(step):
                copy(step, True).wait_recv()
            return jnp.sum(buf[...], axis=0)

        def drain():
            @pl.loop(1, count)
            def _(step):
                copy(step, False).wait_send()

        return finish, drain

    mine = jnp.sum(rhs - outside * swept, keepdims=True)
    part1[my_plane] = jnp.where(lane == 0, mine, jnp.where(lane == 1, diag_sum, 0.0))
    finish1, drain1 = share(part1, a1send, a1recv, plane_group, my_plane, plane_peer)

    both = jnp.concatenate([swept, pltpu.roll(swept, SLOT, 1)], 0)
    spread = select_dot(both, gsum[...], 1)
    for c in range(2):
        for h in range(2):
            values = spread[8 * c : 8 * c + 8, h * H : h * H + H]
            corr[c, h] = jnp.broadcast_to(values[:, None, :], (T, RATIO, H)).reshape(R, H)

    sweep(3)
    part2[ix] = finish1()
    finish2, drain2 = share(part2, a2send, a2recv, nx, ix, line_peer)

    sweep(SWEEPS)

    for f in range(5):
        for d in range(6):
            @pl.when(dirs[d][2])
            def _():
                fine_copy(f, d).wait_send()
    for q in range(2):
        for stage in ("x", "z", "y"):
            coarse_sent(q, stage)
    drain1()

    sums = finish2()
    drain2()
    top = jnp.sum(jnp.where(lane == 0, sums, 0.0), keepdims=True)
    bottom = jnp.sum(jnp.where(lane == 1, sums, 0.0), keepdims=True)
    shift_out[...] = jnp.broadcast_to(top / bottom, (8, 128))


def solution(mesh):
    nx, ny, nz = mesh.shape["gx"], mesh.shape["gy"], mesh.shape["gz"]
    f32, bf16 = jnp.float32, jnp.bfloat16
    dma = pltpu.SemaphoreType.DMA

    def body(*refs):
        kernel(nx, ny, nz, *refs)

    def shards(pressure_start, source, permeability):
        block = pltpu.VMEM((2, D, R, H), f32)
        ghosted = pltpu.VMEM((2, D + 2, R + 2 * TOP, H), f32)
        smoothed, shift = pl.pallas_call(
            body,
            out_shape=(
                jax.ShapeDtypeStruct((D, R, W), f32), jax.ShapeDtypeStruct((8, 128), f32)
            ),
            in_specs=[pl.BlockSpec(memory_space=pltpu.HBM)] * 3,
            out_specs=(
                pl.BlockSpec(memory_space=pltpu.VMEM), pl.BlockSpec(memory_space=pltpu.VMEM)
            ),
            scratch_shapes=[
                ghosted, ghosted, ghosted, ghosted, ghosted,
                block, pltpu.VMEM((2, D + 1, R, H), f32), block, block, block, block, block, block,
                pltpu.VMEM((2, 2, R, H), f32),
                pltpu.VMEM((W, 128), bf16), pltpu.VMEM((W, 128), bf16),
                pltpu.VMEM((2, 2, R, H), f32),
                pltpu.VMEM((5, 2, 8, 128), f32), pltpu.VMEM((5, 2, 8, 128), f32),
                *[
                    pltpu.VMEM(lead + (count, 8, 128), f32)
                    for count in (4, 1)
                    for lead in ((), (2,), (BLOCKS,), (2, BLOCKS - 2))
                ],
                pltpu.VMEM((BLOCKS - 2, 6, 3 * RATIO, 128), f32),
                pltpu.VMEM((ny * nz, 1, 128), f32), pltpu.VMEM((nx, 1, 128), f32),
                dma((3, 2)), dma((5, 6)), dma((5, 6)),
                dma((2, 2)), dma((2, 2)), dma((2, BLOCKS)), dma((2, BLOCKS)), dma((2, 2)), dma((2, 2)),
                dma((ny * nz,)), dma((ny * nz,)), dma((nx,)), dma((nx,)),
            ],
            compiler_params=pltpu.CompilerParams(
                collective_id=0, has_side_effects=True, vmem_limit_bytes=62 << 20
            ),
        )(pressure_start, source, permeability)
        return smoothed + shift[0, 0]

    spec = P("gx", "gy", "gz")
    return jax.shard_map(
        shards, mesh=mesh, in_specs=(spec, spec, spec), out_specs=spec, check_vma=False
    )
```

```python
import functools

import jax
import jax.numpy as jnp
from jax import lax
from jax.experimental import pallas as pl
from jax.experimental.pallas import tpu as pltpu
from jax.sharding import PartitionSpec as P

RATIO = 8
SWEEPS = 4
COARSE_SWEEPS = 8
OMEGA = 0.8
MESH = pl.DeviceIdType.MESH

D, R, W = 16, 64, 256
T = R // RATIO
H = W // 2
TOP = 8
SLOT = 64
FIRST = 8
CX = W // RATIO
REACH = 4
BLOCKS = 2 * REACH + 1
KF = 0
GROUP = 16


def iota(shape, axis):
    return lax.broadcasted_iota(jnp.int32, shape, axis)


def split3(a):
    high = a.astype(jnp.bfloat16)
    rest = a - high.astype(jnp.float32)
    mid = rest.astype(jnp.bfloat16)
    low = (rest - mid.astype(jnp.float32)).astype(jnp.bfloat16)
    return jnp.concatenate([high, mid, low], axis=0)


def select_dot(a, matrix, contract):
    n = a.shape[0]
    b = lax.dot_general(
        split3(a), matrix, (((1,), (contract,)), ((), ())), preferred_element_type=jnp.float32
    )
    return b[:n] + b[n : 2 * n] + b[2 * n :]


def kernel(
    nx, ny, nz,
    p_hbm, s_hbm, k_hbm, out,
    kx, p0, p1, p2, p3, src, wz, wyl, wyh, wxl, wxh, dia, dinv, acc, gsum, gpick, corr,
    xsend, xrecv, own_w, xw, zw, yw, own_f, xf, zf, yf, sides, part1, part2,
    load_sem, fsend, frecv, cxs, cxr, czs, czr, cys, cyr, a1send, a1recv, a2send, a2recv,
):
    ix, iy, iz = lax.axis_index("gx"), lax.axis_index("gy"), lax.axis_index("gz")
    dirs = (
        ("gx", ix - 1, ix > 0), ("gx", ix + 1, ix < nx - 1),
        ("gy", iy - 1, iy > 0), ("gy", iy + 1, iy < ny - 1),
        ("gz", iz - 1, iz > 0), ("gz", iz + 1, iz < nz - 1),
    )
    press = (p0, p1, p2, p3)
    plane_group = ny * nz
    my_plane = iy * nz + iz
    own = pl.ds(TOP, R)
    planes = pl.ds(1, D)

    loads = []
    for n, (ref, place) in enumerate(((k_hbm, kx), (p_hbm, p0), (s_hbm, src))):
        for h in range(2):
            there = place.at[h, planes, own] if n < 2 else place.at[h]
            loads.append(
                pltpu.make_async_copy(ref.at[:, :, pl.ds(h * H, H)], there, load_sem.at[n, h])
            )
    for load in loads:
        load.start()

    barrier = pltpu.get_barrier_semaphore()

    def plane_peer(step):
        other = lax.rem(my_plane + step, plane_group)
        return {"gy": other // nz, "gz": lax.rem(other, nz)}, other

    def line_peer(step):
        other = lax.rem(ix + step, nx)
        return {"gx": other}, other

    for axis, other, exists in dirs:
        @pl.when(exists)
        def _():
            pl.semaphore_signal(barrier, 1, device_id={axis: other}, device_id_type=MESH)

    @pl.loop(1, plane_group)
    def _(step):
        pl.semaphore_signal(barrier, 1, device_id=plane_peer(step)[0], device_id_type=MESH)

    @pl.loop(1, nx)
    def _(step):
        pl.semaphore_signal(barrier, 1, device_id=line_peer(step)[0], device_id_type=MESH)

    near = sum(e.astype(jnp.int32) for _, _, e in dirs)
    lane = iota((1, 128), 1)
    zero_tile = jnp.zeros((8, 128), jnp.float32)
    edge_row = (TOP, TOP + R - 1)
    ghost_row = (TOP - 1, TOP + R)

    for d, (_, _, exists) in enumerate(dirs):
        @pl.when(jnp.logical_not(exists))
        def _():
            for f in range(1, 5):
                if d < 2:
                    press[f - 1][:, d * (D + 1), own] = jnp.zeros((2, R, H), jnp.float32)
                elif d < 4:
                    row = pl.ds(ghost_row[d - 2], 1)
                    press[f - 1][:, planes, row] = jnp.zeros((2, D, 1, H), jnp.float32)
                else:
                    xrecv[f, d - 4] = zero_tile
            if d >= 4:
                for place in (xw, xf):
                    place[d - 4] = jnp.zeros(place.shape[1:], jnp.float32)
            elif d >= 2:
                for place in (yw, yf):
                    place[d - 2] = jnp.zeros(place.shape[1:], jnp.float32)
    far = {}
    for dz in range(-REACH, REACH + 1):
        if dz:
            far[dz] = jnp.logical_and(ix + dz >= 0, ix + dz < nx)

            @pl.when(jnp.logical_not(far[dz]))
            def _():
                for place in (zw, zf):
                    place[dz + REACH] = jnp.zeros(place.shape[1:], jnp.float32)

    acc[...] = jnp.zeros(acc.shape, jnp.float32)

    def fine_copy(f, d, incoming=False):
        axis, other, _ = dirs[d]
        end = d ^ 1
        field = kx if f == KF else press[f - 1]
        if d < 2:
            here = field.at[:, 1 if d == 0 else D, own]
            there = field.at[:, D + 1 if d == 0 else 0, own]
            back = field.at[:, 0 if d == 0 else D + 1, own]
        elif d < 4:
            here = field.at[:, planes, pl.ds(edge_row[d - 2], 1)]
            there = field.at[:, planes, pl.ds(ghost_row[end - 2], 1)]
            back = field.at[:, planes, pl.ds(ghost_row[d - 2], 1)]
        else:
            here, there, back = xsend.at[f, d - 4], xrecv.at[f, end - 4], xrecv.at[f, d - 4]
        return pltpu.make_async_remote_copy(
            src_ref=here,
            dst_ref=back if incoming else there,
            send_sem=fsend.at[f, d],
            recv_sem=frecv.at[f, d if incoming else end],
            device_id={axis: other},
            device_id_type=MESH,
        )

    groups = ((own_w, xw, zw, yw), (own_f, xf, zf, yf))

    def coarse_copy(q, stage, way, incoming=False):
        own_q, x_q, z_q, y_q = groups[q]
        if stage == "z":
            here, place = z_q.at[REACH], z_q
            slot = REACH + way if incoming else REACH - way
            sems, to = (czs, czr), {"gx": ix + way}
            sent = REACH + way
        else:
            axis, other, _ = dirs[(4 if stage == "x" else 2) + way]
            here, place = (own_q, x_q) if stage == "x" else (z_q.at[pl.ds(1, BLOCKS - 2)], y_q)
            slot = way if incoming else 1 - way
            sems, to = (cxs, cxr) if stage == "x" else (cys, cyr), {axis: other}
            sent = way
        return pltpu.make_async_remote_copy(
            src_ref=here, dst_ref=place.at[slot], send_sem=sems[0].at[q, sent],
            recv_sem=sems[1].at[q, slot], device_id=to, device_id_type=MESH,
        )

    def ways(stage):
        if stage == "z":
            return list(far.items())
        first = 4 if stage == "x" else 2
        return [(way, dirs[first + way][2]) for way in range(2)]

    def coarse_start(q, stage):
        for way, exists in ways(stage):
            @pl.when(exists)
            def _():
                coarse_copy(q, stage, way).start()

    def coarse_arrive(q, stage):
        for way, exists in ways(stage):
            @pl.when(exists)
            def _():
                coarse_copy(q, stage, way, True).wait_recv()

    def coarse_sent(q, stage):
        for way, exists in ways(stage):
            @pl.when(exists)
            def _():
                coarse_copy(q, stage, way).wait_send()

    def start(make, f, which):
        for d in which:
            @pl.when(dirs[d][2])
            def _():
                make(f, d).start()

    def arrive(make, f, which):
        for d in which:
            @pl.when(dirs[d][2])
            def _():
                make(f, d, True).wait_recv()

    def edges_of(news, g, at_z, low, high):
        n = GROUP // 8
        for t in range(g * n, g * n + n):
            to = 16 * t + at_z
            part = slice(8 * (t - g * n), 8 * (t - g * n) + 8)
            left, right = news[0][part], news[1][part]
            low = jnp.where(lane == to, pltpu.roll(left, to, 1) if to else left, low)
            high = jnp.where(
                lane == to, pltpu.roll(right, to + 1, 1) if to < 127 else right, high
            )
        return low, high

    def keep_packed(f, faces):
        xsend[f, 0] = faces[0]
        xsend[f, 1] = faces[1]

    def ghosts(f, base):
        back = lax.rem(128 - base, 128) if not isinstance(base, int) else (128 - base) % 128
        low, high = xrecv[f, 0], xrecv[f, 1]
        if not isinstance(base, int) or base:
            low, high = pltpu.roll(low, back, 1), pltpu.roll(high, back, 1)

        def turn(v, by):
            return pltpu.roll(v, by % 128, 1) if by % 128 else v

        return (
            lambda at, t: turn(low, 128 - 16 * t - at),
            lambda at, t: turn(high, 255 - 16 * t - at),
        )

    def around(field, z, g, at_z, makers):
        n = GROUP // 8
        lows, highs = [
            jnp.concatenate([make(at_z, t) for t in range(g * n, g * n + n)], 0) for make in makers
        ]
        at = TOP + g * GROUP
        own_rows = [field[h, z + 1, pl.ds(at, GROUP), :] for h in range(2)]
        low_y = [field[h, z + 1, pl.ds(at - 1, GROUP), :] for h in range(2)]
        high_y = [field[h, z + 1, pl.ds(at + 1, GROUP), :] for h in range(2)]
        rl, rr = [pltpu.roll(v, 1, 1) for v in own_rows]
        low_x = [jnp.where(lane == 0, lows, rl), jnp.where(lane == 0, rl, rr)]
        sl, sr = [pltpu.roll(v, H - 1, 1) for v in own_rows]
        high_x = [jnp.where(lane == H - 1, sr, sl), jnp.where(lane == H - 1, highs, sr)]
        return own_rows, low_y, high_y, low_x, high_x

    def pack_field(field):
        def pack(i, faces):
            z = 4 * i
            fresh = (zero_tile, zero_tile)
            for j in range(4):
                for g in range(R // GROUP):
                    at = pl.ds(TOP + g * GROUP, GROUP)
                    rows = [field[h, z + 1 + j, at, :] for h in range(2)]
                    fresh = edges_of(rows, g, j, *fresh)
            mine = lax.rem(lane, 16) // 4 == i
            return tuple(jnp.where(mine, pltpu.roll(a, z, 1), b) for a, b in zip(fresh, faces))

        return lax.fori_loop(0, D // 4, pack, (zero_tile, zero_tile))

    for load in loads[:2]:
        load.wait()
    keep_packed(KF, pack_field(kx))
    pl.semaphore_wait(barrier, near + (plane_group - 1) + (nx - 1))
    start(fine_copy, KF, (4, 5, 2, 3, 0, 1))
    for load in loads[2:4]:
        load.wait()
    keep_packed(1, pack_field(p0))
    start(fine_copy, 1, (4, 5, 2, 3, 0, 1))

    for d, (_, _, exists) in enumerate(dirs):
        @pl.when(jnp.logical_not(exists))
        def _():
            if d < 2:
                kx[:, d * (D + 1), own] = kx[:, 1 + d * (D - 1), own]
            elif d < 4:
                kx[:, planes, pl.ds(ghost_row[d - 2], 1)] = kx[:, planes, pl.ds(edge_row[d - 2], 1)]
            else:
                xrecv[KF, d - 4] = xsend[KF, d - 4]

    column, spot = iota((W, 128), 0), iota((W, 128), 1)
    home = spot == FIRST + column // RATIO
    gsum[...] = jnp.where(home, 1.0, 0.0).astype(jnp.bfloat16)
    gpick[...] = jnp.where(
        jnp.logical_and(home, lax.rem(column, RATIO) == 0), 1.0, 0.0
    ).astype(jnp.bfloat16)

    arrive(fine_copy, KF, range(2, 6))

    def weigh(base, offsets):
        makers = ghosts(KF, base)
        for at_z in offsets:
            z = base + at_z
            for g in range(R // GROUP):
                rows = pl.ds(g * GROUP, GROUP)
                k, *others = around(kx, z, g, at_z, makers)
                for h in range(2):
                    at = pl.ds(TOP + g * GROUP, GROUP)
                    half = 0.5 * k[h]
                    low_z = half + 0.5 * kx[h, z, at, :]
                    high_z = half + 0.5 * kx[h, z + 2, at, :]
                    total = low_z + high_z
                    wz[h, z, rows, :] = low_z
                    for ref, other in zip((wyl, wyh, wxl, wxh), others):
                        face = half + 0.5 * other[h]
                        ref[h, z, rows, :] = face
                        total = total + face
                    dia[h, z, rows, :] = total
                    dinv[h, z, rows, :] = OMEGA / total

    @pl.loop(0, D // 2 - 1)
    def _(i):
        weigh(2 * i + 1, (0, 1))

    arrive(fine_copy, KF, (0, 1))
    weigh(0, (0, D - 1))
    for h in range(2):
        wz[h, D] = 0.5 * (kx[h, D, own, :] + kx[h, D + 1, own, :])

    def tile_sum(plane):
        return jnp.sum(plane.reshape(T, RATIO, H), axis=1)

    def wide(parts):
        return jnp.concatenate(parts, axis=1)

    def halves(make):
        return wide([make(0), make(1)])

    def sum_planes(c, load):
        total = load(RATIO * c)
        for z in range(RATIO * c + 1, RATIO * c + RATIO):
            total = total + load(z)
        return total

    def every(ref, h, c, first):
        return sum_planes(c, lambda z: ref[h, z, pl.ds(first, T, stride=RATIO), :])

    summed, picked, last = [], [], []
    for c in range(2):
        summed += [
            halves(lambda h: tile_sum(wz[h, RATIO * c])),
            halves(lambda h: tile_sum(wz[h, RATIO * c + RATIO])),
            halves(lambda h: every(wyl, h, c, 0)),
            halves(lambda h: every(wyh, h, c, RATIO - 1)),
        ]
        picked.append(halves(lambda h: tile_sum(sum_planes(c, lambda z: wxl[h, z]))))
        last.append(tile_sum(sum_planes(c, lambda z: wxh[1, z])))
    sums = select_dot(jnp.concatenate(summed, 0), gsum[...], 0)
    picks = select_dot(jnp.concatenate(picked, 0), gpick[...], 0)

    def pair(low, high):
        return low + pltpu.roll(high, SLOT, 1)

    zl, zh, yl, yh = [pair(sums[8 * n : 8 * n + 8], sums[8 * n + 32 : 8 * n + 40]) for n in range(4)]
    xl = pair(picks[:8], picks[8:])
    inside = lax.rem(lane, SLOT)
    final_lane = FIRST + CX - 1
    xh = pltpu.roll(xl, 127, 1)
    for c in range(2):
        to = c * SLOT + final_lane
        xh = jnp.where(lane == to, pltpu.roll(last[c], (to + 1) % 128, 1), xh)
    valid = jnp.logical_and(inside >= FIRST, inside <= final_lane)
    xh = jnp.where(valid, xh, 0.0)
    cdiag = zl + zh + yl + yh + xl + xh
    scale = jnp.where(valid, OMEGA / jnp.where(valid, cdiag, 1.0), 0.0)
    weights = (zl, zh, yl, yh, xl, xh)
    for n, field in enumerate((zl, yl, xl, scale)):
        own_w[n] = field
    coarse_start(0, "x")
    tile_row = iota((8, 1), 0)
    even = lane < SLOT
    edges = (
        even, jnp.logical_not(even), tile_row == 0, tile_row == 7,
        inside == FIRST, inside == final_lane,
    )
    outside = zero_tile
    for (_, _, exists), edge, w in zip(dirs, edges, weights):
        gone = jnp.where(exists, 0.0, 1.0)
        outside = outside + jnp.where(edge, gone * w, 0.0)
    diag_sum = jnp.sum(cdiag, keepdims=True)

    def merge(q):
        own_q, x_q, z_q, _ = groups[q]
        for n in range(own_q.shape[0]):
            low, high = pltpu.roll(x_q[0, n], 128 - CX, 1), pltpu.roll(x_q[1, n], CX, 1)
            after = jnp.logical_and(inside > final_lane, inside <= final_lane + RATIO)
            z_q[REACH, n] = jnp.where(inside < FIRST, low, jnp.where(after, high, own_q[n]))

    def push_weights():
        coarse_arrive(0, "x")
        merge(0)
        coarse_start(0, "z")

    loads[4].wait()
    loads[5].wait()

    def sweep_planes(n, base, offsets, faces):
        field = press[n - 1]
        makers = ghosts(n, base)
        low, high = zero_tile, zero_tile
        fresh = []
        for at_z in offsets:
            z = base + at_z
            for g in range(R // GROUP):
                rows = pl.ds(g * GROUP, GROUP)
                v, *others = around(field, z, g, at_z, makers)
                news = []
                for h in range(2):
                    at = pl.ds(TOP + g * GROUP, GROUP)
                    flux = src[h, z, rows, :] + wz[h, z, rows, :] * field[h, z, at, :]
                    flux = flux + wz[h, z + 1, rows, :] * field[h, z + 2, at, :]
                    for ref, other in zip((wyl, wyh, wxl, wxh), others):
                        flux = flux + ref[h, z, rows, :] * other[h]
                    if n == 1:
                        acc[h, z // RATIO, rows, :] += flux - dia[h, z, rows, :] * v[h]
                    new = (1.0 - OMEGA) * v[h] + dinv[h, z, rows, :] * flux
                    if n < SWEEPS:
                        press[n][h, z + 1, at, :] = new
                        news.append(new)
                    else:
                        out[z, rows, pl.ds(h * H, H)] = new + corr[z // RATIO, h, rows, :]
                if n < SWEEPS:
                    fresh.append((news, g, at_z))
        if n == SWEEPS:
            return faces
        for news, g, at_z in fresh:
            low, high = edges_of(news, g, at_z, low, high)
        place = lax.rem(lane, 16)
        if isinstance(base, int):
            mine = functools.reduce(jnp.logical_or, [place == base + at_z for at_z in offsets])
        else:
            low, high = pltpu.roll(low, base, 1), pltpu.roll(high, base, 1)
            mine = jnp.logical_and(place >= base + offsets[0], place <= base + offsets[-1])
        return jnp.where(mine, low, faces[0]), jnp.where(mine, high, faces[1])

    none = (zero_tile, zero_tile)
    rim = (0, D - 1)

    def sweep(n):
        def inner(i, faces):
            return sweep_planes(n, 2 * i + 1, (0, 1), faces)

        count = D // 2 - 1
        if n == 1:
            arrive(fine_copy, n, range(2, 6))
            faces = lax.fori_loop(0, count, inner, none)
            arrive(fine_copy, n, (0, 1))
            keep_packed(n + 1, sweep_planes(n, 0, rim, faces))
            return
        arrive(fine_copy, n, range(6))
        faces = sweep_planes(n, 0, rim, none)
        if n < SWEEPS:
            faces = lax.fori_loop(0, 1, inner, faces)
            start(fine_copy, n + 1, (0, 1))
        faces = lax.fori_loop(1 if n < SWEEPS else 0, count, inner, faces)
        if n < SWEEPS:
            keep_packed(n + 1, faces)
            start(fine_copy, n + 1, (4, 5, 2, 3))

    sweep(1)

    resid = select_dot(
        jnp.concatenate([halves(lambda h: tile_sum(acc[h, c])) for c in range(2)], 0), gsum[...], 0
    )
    rhs = pair(resid[:8], resid[8:])
    fixed = scale * rhs

    own_f[0] = fixed
    coarse_start(1, "x")
    start(fine_copy, 2, (4, 5, 2, 3, 0, 1))
    push_weights()

    coarse_arrive(1, "x")
    merge(1)
    coarse_start(1, "z")
    for q in range(2):
        coarse_arrive(q, "z")
        coarse_start(q, "y")

    sweep(2)

    def extended(q, b, n):
        _, _, z_q, y_q = groups[q]
        if b in (0, BLOCKS - 1):
            return jnp.concatenate([zero_tile, z_q[b, n], zero_tile], 0)
        return jnp.concatenate([y_q[0, b - 1, n], z_q[b, n], y_q[1, b - 1, n]], 0)

    def other_slot(v):
        return pltpu.roll(v, SLOT, 1)

    coarse_arrive(0, "y")
    turned = [other_slot(extended(0, b, 0)) for b in range(BLOCKS)]
    tall = 3 * RATIO
    for b in range(1, BLOCKS - 1):
        wz_b, wy_b, wx_b, scale_b = [extended(0, b, n) for n in range(4)]
        high = (
            jnp.where(even, turned[b], turned[b + 1]),
            pltpu.roll(wy_b, tall - 1, 0),
            pltpu.roll(wx_b, 127, 1),
        )
        for n, w in enumerate((wz_b, high[0], wy_b, high[1], wx_b, high[2])):
            sides[b - 1, n] = scale_b * w

    coarse_arrive(1, "y")
    start_values = [extended(1, b, 0) for b in range(BLOCKS)]
    e = list(start_values)
    for m in range(1, COARSE_SWEEPS):
        turned = [other_slot(v) for v in e]
        following = list(e)
        for b in range(1, BLOCKS - 1):
            if 2 * abs(b - REACH) - 1 > COARSE_SWEEPS - 1 - m:
                continue
            beside = (
                jnp.where(even, turned[b - 1], turned[b]),
                jnp.where(even, turned[b], turned[b + 1]),
                pltpu.roll(e[b], 1, 0),
                pltpu.roll(e[b], tall - 1, 0),
                pltpu.roll(e[b], 1, 1),
                pltpu.roll(e[b], 127, 1),
            )
            new = (1.0 - OMEGA) * e[b] + start_values[b]
            for n, g in enumerate(beside):
                new = new + sides[b - 1, n] * g
            following[b] = new
        e = following
    swept = e[REACH][RATIO : 2 * RATIO]

    def share(buf, ssem, rsem, count, me, peer_of):
        def copy(step, incoming):
            peer, other = peer_of(step)
            return pltpu.make_async_remote_copy(
                src_ref=buf.at[me], dst_ref=buf.at[other if incoming else me],
                send_sem=ssem.at[other], recv_sem=rsem.at[other if incoming else me],
                device_id=peer, device_id_type=MESH,
            )

        @pl.loop(1, count)
        def _(step):
            copy(step, False).start()

        def finish():
            @pl.loop(1, count)
            def _(step):
                copy(step, True).wait_recv()
            return jnp.sum(buf[...], axis=0)

        def drain():
            @pl.loop(1, count)
            def _(step):
                copy(step, False).wait_send()

        return finish, drain

    mine = jnp.sum(rhs - outside * swept, keepdims=True)
    part1[my_plane] = jnp.where(lane == 0, mine, jnp.where(lane == 1, diag_sum, 0.0))
    finish1, drain1 = share(part1, a1send, a1recv, plane_group, my_plane, plane_peer)

    both = jnp.concatenate([swept, pltpu.roll(swept, SLOT, 1)], 0)
    spread = select_dot(both, gsum[...], 1)
    for c in range(2):
        for h in range(2):
            values = spread[8 * c : 8 * c + 8, h * H : h * H + H]
            corr[c, h] = jnp.broadcast_to(values[:, None, :], (T, RATIO, H)).reshape(R, H)

    sweep(3)
    part2[ix] = finish1()
    finish2, drain2 = share(part2, a2send, a2recv, nx, ix, line_peer)

    sweep(SWEEPS)

    for f in range(5):
        for d in range(6):
            @pl.when(dirs[d][2])
            def _():
                fine_copy(f, d).wait_send()
    for q in range(2):
        for stage in ("x", "z", "y"):
            coarse_sent(q, stage)
    drain1()

    sums = finish2()
    drain2()
    top = jnp.sum(jnp.where(lane == 0, sums, 0.0), keepdims=True)
    bottom = jnp.sum(jnp.where(lane == 1, sums, 0.0), keepdims=True)
    shift = top / bottom

    @pl.loop(0, D // 4)
    def _(i):
        for j in range(4):
            out[4 * i + j] = out[4 * i + j] + shift


def solution(mesh):
    nx, ny, nz = mesh.shape["gx"], mesh.shape["gy"], mesh.shape["gz"]
    f32, bf16 = jnp.float32, jnp.bfloat16
    dma = pltpu.SemaphoreType.DMA

    def body(*refs):
        kernel(nx, ny, nz, *refs)

    def shards(*arrays):
        block = pltpu.VMEM((2, D, R, H), f32)
        ghosted = pltpu.VMEM((2, D + 2, R + 2 * TOP, H), f32)
        return pl.pallas_call(
            body,
            out_shape=jax.ShapeDtypeStruct((D, R, W), f32),
            in_specs=[pl.BlockSpec(memory_space=pltpu.HBM)] * 3,
            out_specs=pl.BlockSpec(memory_space=pltpu.VMEM),
            scratch_shapes=[
                ghosted, ghosted, ghosted, ghosted, ghosted,
                block, pltpu.VMEM((2, D + 1, R, H), f32), block, block, block, block, block, block,
                pltpu.VMEM((2, 2, R, H), f32),
                pltpu.VMEM((W, 128), bf16), pltpu.VMEM((W, 128), bf16),
                pltpu.VMEM((2, 2, R, H), f32),
                pltpu.VMEM((5, 2, 8, 128), f32), pltpu.VMEM((5, 2, 8, 128), f32),
                *[
                    pltpu.VMEM(lead + (count, 8, 128), f32)
                    for count in (4, 1)
                    for lead in ((), (2,), (BLOCKS,), (2, BLOCKS - 2))
                ],
                pltpu.VMEM((BLOCKS - 2, 6, 3 * RATIO, 128), f32),
                pltpu.VMEM((ny * nz, 1, 128), f32), pltpu.VMEM((nx, 1, 128), f32),
                dma((3, 2)), dma((5, 6)), dma((5, 6)),
                dma((2, 2)), dma((2, 2)), dma((2, BLOCKS)), dma((2, BLOCKS)), dma((2, 2)), dma((2, 2)),
                dma((ny * nz,)), dma((ny * nz,)), dma((nx,)), dma((nx,)),
            ],
            compiler_params=pltpu.CompilerParams(
                collective_id=0, has_side_effects=True, vmem_limit_bytes=40 << 20
            ),
        )(*[pltpu.with_memory_space_constraint(a, pltpu.HBM) for a in arrays])

    spec = P("gx", "gy", "gz")
    return jax.shard_map(
        shards, mesh=mesh, in_specs=(spec, spec, spec), out_specs=spec, check_vma=False
    )
```

```python
import functools

import jax
import jax.numpy as jnp
from jax import lax
from jax.experimental import pallas as pl
from jax.experimental.pallas import tpu as pltpu
from jax.sharding import PartitionSpec as P

RATIO = 8
SWEEPS = 4
COARSE_SWEEPS = 8
OMEGA = 0.8
MESH = pl.DeviceIdType.MESH

D, R, W = 16, 64, 256
T = R // RATIO
H = W // 2
TOP = 8
SLOT = 64
FIRST = 8
CX = W // RATIO
REACH = 4
BLOCKS = 2 * REACH + 1
KF = 0
CHUNK = R // 2
GROUP = 16


def iota(shape, axis):
    return lax.broadcasted_iota(jnp.int32, shape, axis)


def split3(a):
    high = a.astype(jnp.bfloat16)
    rest = a - high.astype(jnp.float32)
    mid = rest.astype(jnp.bfloat16)
    low = (rest - mid.astype(jnp.float32)).astype(jnp.bfloat16)
    return jnp.concatenate([high, mid, low], axis=0)


def select_dot(a, matrix, contract):
    n = a.shape[0]
    b = lax.dot_general(
        split3(a), matrix, (((1,), (contract,)), ((), ())), preferred_element_type=jnp.float32
    )
    return b[:n] + b[n : 2 * n] + b[2 * n :]


def kernel(
    nx, ny, nz,
    p_hbm, s_hbm, k_hbm, out,
    kx, p0, p1, p2, p3, src, wz, wyl, wyh, wxl, wxh, dia, dinv, acc, gsum, gpick, corr,
    xsend, xrecv, own_w, xw, zw, yw, own_f, xf, zf, yf, sides, part1, part2,
    load_sem, fsend, frecv, cxs, cxr, czs, czr, cys, cyr, a1send, a1recv, a2send, a2recv,
):
    ix, iy, iz = lax.axis_index("gx"), lax.axis_index("gy"), lax.axis_index("gz")
    dirs = (
        ("gx", ix - 1, ix > 0), ("gx", ix + 1, ix < nx - 1),
        ("gy", iy - 1, iy > 0), ("gy", iy + 1, iy < ny - 1),
        ("gz", iz - 1, iz > 0), ("gz", iz + 1, iz < nz - 1),
    )
    press = (p0, p1, p2, p3)
    plane_group = ny * nz
    my_plane = iy * nz + iz
    own = pl.ds(TOP, R)
    planes = pl.ds(1, D)

    loads = []
    for n, (ref, place) in enumerate(((k_hbm, kx), (p_hbm, p0), (s_hbm, src))):
        for h in range(2):
            there = place.at[h, planes, own] if n < 2 else place.at[h]
            loads.append(
                pltpu.make_async_copy(ref.at[:, :, pl.ds(h * H, H)], there, load_sem.at[n, h])
            )
    for load in loads:
        load.start()

    barrier = pltpu.get_barrier_semaphore()

    plane_peers = [
        {"gy": lax.rem(iy + dy, ny), "gz": lax.rem(iz + dz, nz)}
        for dy in range(ny) for dz in range(nz) if dy or dz
    ]
    line_peers = [{"gx": lax.rem(ix + step, nx)} for step in range(1, nx)]

    for axis, other, exists in dirs:
        @pl.when(exists)
        def _():
            pl.semaphore_signal(barrier, 1, device_id={axis: other}, device_id_type=MESH)

    for peer in plane_peers + line_peers:
        pl.semaphore_signal(barrier, 1, device_id=peer, device_id_type=MESH)

    near = sum(e.astype(jnp.int32) for _, _, e in dirs)
    lane = iota((1, 128), 1)
    zero_tile = jnp.zeros((8, 128), jnp.float32)
    edge_row = (TOP, TOP + R - 1)
    ghost_row = (TOP - 1, TOP + R)

    for d, (_, _, exists) in enumerate(dirs):
        @pl.when(jnp.logical_not(exists))
        def _():
            for f in range(1, 5):
                if d < 2:
                    press[f - 1][:, d * (D + 1), own] = jnp.zeros((2, R, H), jnp.float32)
                elif d < 4:
                    row = pl.ds(ghost_row[d - 2], 1)
                    press[f - 1][:, planes, row] = jnp.zeros((2, D, 1, H), jnp.float32)
                else:
                    xrecv[f, d - 4] = zero_tile
            if d >= 4:
                for place in (xw, xf):
                    place[d - 4] = jnp.zeros(place.shape[1:], jnp.float32)
            elif d >= 2:
                for place in (yw, yf):
                    place[d - 2] = jnp.zeros(place.shape[1:], jnp.float32)
    far = {}
    for dz in range(-REACH, REACH + 1):
        if dz:
            far[dz] = jnp.logical_and(ix + dz >= 0, ix + dz < nx)

            @pl.when(jnp.logical_not(far[dz]))
            def _():
                for place in (zw, zf):
                    place[dz + REACH] = jnp.zeros(place.shape[1:], jnp.float32)

    acc[...] = jnp.zeros(acc.shape, jnp.float32)

    def fine_copy(f, d, incoming=False):
        chunk, d = d // 6, d % 6
        axis, other, _ = dirs[d]
        rows = pl.ds(TOP + chunk * CHUNK, CHUNK)
        shift = 6 * chunk
        end = d ^ 1
        field = kx if f == KF else press[f - 1]
        if d < 2:
            here = field.at[:, 1 if d == 0 else D, rows]
            there = field.at[:, D + 1 if d == 0 else 0, rows]
            back = field.at[:, 0 if d == 0 else D + 1, rows]
        elif d < 4:
            here = field.at[:, planes, pl.ds(edge_row[d - 2], 1)]
            there = field.at[:, planes, pl.ds(ghost_row[end - 2], 1)]
            back = field.at[:, planes, pl.ds(ghost_row[d - 2], 1)]
        else:
            here, there, back = xsend.at[f, d - 4], xrecv.at[f, end - 4], xrecv.at[f, d - 4]
        return pltpu.make_async_remote_copy(
            src_ref=here,
            dst_ref=back if incoming else there,
            send_sem=fsend.at[f, d + shift],
            recv_sem=frecv.at[f, (d if incoming else end) + shift],
            device_id={axis: other},
            device_id_type=MESH,
        )

    groups = ((own_w, xw, zw, yw), (own_f, xf, zf, yf))

    def coarse_copy(q, stage, way, incoming=False):
        own_q, x_q, z_q, y_q = groups[q]
        if stage == "z":
            slot = REACH + way if incoming else REACH - way
            here, there = z_q.at[REACH], z_q.at[slot]
            if q == 0 and abs(way) == REACH:
                here, there = here.at[pl.ds(0, 1)], there.at[pl.ds(0, 1)]
            sems, to = (czs, czr), {"gx": ix + way}
            sent = REACH + way
        else:
            piece, side = way // 2, way % 2
            axis, other, _ = dirs[(4 if stage == "x" else 2) + side]
            slot = way if incoming else way ^ 1
            if stage == "x":
                here, there, sems = own_q, x_q.at[slot], (cxs, cxr)
            else:
                first, size = ((REACH - 2, 3), (0, REACH - 2), (REACH + 1, REACH - 2))[piece]
                here = z_q.at[pl.ds(first + 1, size)]
                there = y_q.at[slot % 2, pl.ds(first, size)]
                sems = (cys, cyr)
            to, sent = {axis: other}, way
        return pltpu.make_async_remote_copy(
            src_ref=here, dst_ref=there, send_sem=sems[0].at[q, sent],
            recv_sem=sems[1].at[q, slot], device_id=to, device_id_type=MESH,
        )

    def ways(q, stage, incoming):
        if stage == "z":
            useless = (-REACH if incoming else REACH) if q == 0 else 0
            return [(way, exists) for way, exists in far.items() if way != useless]
        first = 4 if stage == "x" else 2
        return [(way, dirs[first + way % 2][2]) for way in range(2 if stage == "x" else 6)]

    def coarse_start(q, stage, only=None):
        for way, exists in ways(q, stage, False):
            if only is not None and way not in only:
                continue

            @pl.when(exists)
            def _():
                coarse_copy(q, stage, way).start()

    def coarse_arrive(q, stage, only=None):
        for way, exists in ways(q, stage, True):
            if only is not None and way not in only:
                continue

            @pl.when(exists)
            def _():
                coarse_copy(q, stage, way, True).wait_recv()

    def coarse_sent(q, stage):
        for way, exists in ways(q, stage, False):
            @pl.when(exists)
            def _():
                coarse_copy(q, stage, way).wait_send()

    def start(make, f, which):
        for d in which:
            @pl.when(dirs[d % 6][2])
            def _():
                make(f, d).start()

    def arrive(make, f, which):
        for d in which:
            @pl.when(dirs[d % 6][2])
            def _():
                make(f, d, True).wait_recv()

    def edges_of(news, g, at_z, low, high):
        n = GROUP // 8
        for t in range(g * n, g * n + n):
            to = 16 * t + at_z
            part = slice(8 * (t - g * n), 8 * (t - g * n) + 8)
            left, right = news[0][part], news[1][part]
            low = jnp.where(lane == to, pltpu.roll(left, to, 1) if to else left, low)
            high = jnp.where(
                lane == to, pltpu.roll(right, to + 1, 1) if to < 127 else right, high
            )
        return low, high

    def keep_packed(f, faces):
        xsend[f, 0] = faces[0]
        xsend[f, 1] = faces[1]

    def ghosts(f, base):
        back = lax.rem(128 - base, 128) if not isinstance(base, int) else (128 - base) % 128
        low, high = xrecv[f, 0], xrecv[f, 1]
        if not isinstance(base, int) or base:
            low, high = pltpu.roll(low, back, 1), pltpu.roll(high, back, 1)

        def turn(v, by):
            return pltpu.roll(v, by % 128, 1) if by % 128 else v

        return (
            lambda at, t: turn(low, 128 - 16 * t - at),
            lambda at, t: turn(high, 255 - 16 * t - at),
        )

    def around(field, z, g, at_z, makers):
        n = GROUP // 8
        lows, highs = [
            jnp.concatenate([make(at_z, t) for t in range(g * n, g * n + n)], 0) for make in makers
        ]
        at = TOP + g * GROUP
        own_rows = [field[h, z + 1, pl.ds(at, GROUP), :] for h in range(2)]
        low_y = [field[h, z + 1, pl.ds(at - 1, GROUP), :] for h in range(2)]
        high_y = [field[h, z + 1, pl.ds(at + 1, GROUP), :] for h in range(2)]
        rl, rr = [pltpu.roll(v, 1, 1) for v in own_rows]
        low_x = [jnp.where(lane == 0, lows, rl), jnp.where(lane == 0, rl, rr)]
        sl, sr = [pltpu.roll(v, H - 1, 1) for v in own_rows]
        high_x = [jnp.where(lane == H - 1, sr, sl), jnp.where(lane == H - 1, highs, sr)]
        return own_rows, low_y, high_y, low_x, high_x

    def pack_field(field):
        def pack(i, faces):
            z = 4 * i
            fresh = (zero_tile, zero_tile)
            for j in range(4):
                for g in range(R // GROUP):
                    at = pl.ds(TOP + g * GROUP, GROUP)
                    rows = [field[h, z + 1 + j, at, :] for h in range(2)]
                    fresh = edges_of(rows, g, j, *fresh)
            mine = lax.rem(lane, 16) // 4 == i
            return tuple(jnp.where(mine, pltpu.roll(a, z, 1), b) for a, b in zip(fresh, faces))

        return lax.fori_loop(0, D // 4, pack, (zero_tile, zero_tile))

    for load in loads[:2]:
        load.wait()
    keep_packed(KF, pack_field(kx))
    pl.semaphore_wait(barrier, near + (plane_group - 1) + (nx - 1))
    start(fine_copy, KF, (4, 5, 2, 3, 0, 1, 6, 7))
    for load in loads[2:4]:
        load.wait()
    keep_packed(1, pack_field(p0))
    start(fine_copy, 1, (4, 5, 2, 3, 0, 1, 6, 7))

    for d, (_, _, exists) in enumerate(dirs):
        @pl.when(jnp.logical_not(exists))
        def _():
            if d < 2:
                kx[:, d * (D + 1), own] = kx[:, 1 + d * (D - 1), own]
            elif d < 4:
                kx[:, planes, pl.ds(ghost_row[d - 2], 1)] = kx[:, planes, pl.ds(edge_row[d - 2], 1)]
            else:
                xrecv[KF, d - 4] = xsend[KF, d - 4]

    column, spot = iota((W, 128), 0), iota((W, 128), 1)
    home = spot == FIRST + column // RATIO
    gsum[...] = jnp.where(home, 1.0, 0.0).astype(jnp.bfloat16)
    gpick[...] = jnp.where(
        jnp.logical_and(home, lax.rem(column, RATIO) == 0), 1.0, 0.0
    ).astype(jnp.bfloat16)

    arrive(fine_copy, KF, range(2, 6))

    def weigh(base, offsets):
        makers = ghosts(KF, base)
        for at_z in offsets:
            z = base + at_z
            for g in range(R // GROUP):
                rows = pl.ds(g * GROUP, GROUP)
                k, *others = around(kx, z, g, at_z, makers)
                for h in range(2):
                    at = pl.ds(TOP + g * GROUP, GROUP)
                    half = 0.5 * k[h]
                    low_z = half + 0.5 * kx[h, z, at, :]
                    high_z = half + 0.5 * kx[h, z + 2, at, :]
                    total = low_z + high_z
                    wz[h, z, rows, :] = low_z
                    for ref, other in zip((wyl, wyh, wxl, wxh), others):
                        face = half + 0.5 * other[h]
                        ref[h, z, rows, :] = face
                        total = total + face
                    dia[h, z, rows, :] = total
                    dinv[h, z, rows, :] = OMEGA / total

    @pl.loop(0, D // 2 - 1)
    def _(i):
        weigh(2 * i + 1, (0, 1))

    arrive(fine_copy, KF, (0, 1, 6, 7))
    weigh(0, (0, D - 1))
    for h in range(2):
        wz[h, D] = 0.5 * (kx[h, D, own, :] + kx[h, D + 1, own, :])

    def tile_sum(plane):
        return jnp.sum(plane.reshape(T, RATIO, H), axis=1)

    def wide(parts):
        return jnp.concatenate(parts, axis=1)

    def halves(make):
        return wide([make(0), make(1)])

    def sum_planes(c, load):
        total = load(RATIO * c)
        for z in range(RATIO * c + 1, RATIO * c + RATIO):
            total = total + load(z)
        return total

    def every(ref, h, c, first):
        return sum_planes(c, lambda z: ref[h, z, pl.ds(first, T, stride=RATIO), :])

    summed, picked, last = [], [], []
    for c in range(2):
        summed += [
            halves(lambda h: tile_sum(wz[h, RATIO * c])),
            halves(lambda h: tile_sum(wz[h, RATIO * c + RATIO])),
            halves(lambda h: every(wyl, h, c, 0)),
            halves(lambda h: every(wyh, h, c, RATIO - 1)),
        ]
        picked.append(halves(lambda h: tile_sum(sum_planes(c, lambda z: wxl[h, z]))))
        last.append(tile_sum(sum_planes(c, lambda z: wxh[1, z])))
    sums = select_dot(jnp.concatenate(summed, 0), gsum[...], 0)
    picks = select_dot(jnp.concatenate(picked, 0), gpick[...], 0)

    def pair(low, high):
        return low + pltpu.roll(high, SLOT, 1)

    zl, zh, yl, yh = [pair(sums[8 * n : 8 * n + 8], sums[8 * n + 32 : 8 * n + 40]) for n in range(4)]
    xl = pair(picks[:8], picks[8:])
    inside = lax.rem(lane, SLOT)
    final_lane = FIRST + CX - 1
    xh = pltpu.roll(xl, 127, 1)
    for c in range(2):
        to = c * SLOT + final_lane
        xh = jnp.where(lane == to, pltpu.roll(last[c], (to + 1) % 128, 1), xh)
    valid = jnp.logical_and(inside >= FIRST, inside <= final_lane)
    xh = jnp.where(valid, xh, 0.0)
    cdiag = zl + zh + yl + yh + xl + xh
    scale = jnp.where(valid, OMEGA / jnp.where(valid, cdiag, 1.0), 0.0)
    weights = (zl, zh, yl, yh, xl, xh)
    for n, field in enumerate((zl, yl, xl, scale)):
        own_w[n] = field
    coarse_start(0, "x")
    tile_row = iota((8, 1), 0)
    even = lane < SLOT
    edges = (
        even, jnp.logical_not(even), tile_row == 0, tile_row == 7,
        inside == FIRST, inside == final_lane,
    )
    outside = zero_tile
    for (_, _, exists), edge, w in zip(dirs, edges, weights):
        gone = jnp.where(exists, 0.0, 1.0)
        outside = outside + jnp.where(edge, gone * w, 0.0)
    diag_sum = jnp.sum(cdiag, keepdims=True)

    def merge(q):
        own_q, x_q, z_q, _ = groups[q]
        for n in range(own_q.shape[0]):
            low, high = pltpu.roll(x_q[0, n], 128 - CX, 1), pltpu.roll(x_q[1, n], CX, 1)
            after = jnp.logical_and(inside > final_lane, inside <= final_lane + RATIO)
            z_q[REACH, n] = jnp.where(inside < FIRST, low, jnp.where(after, high, own_q[n]))

    def push_weights():
        coarse_arrive(0, "x")
        merge(0)
        coarse_start(0, "z")

    loads[4].wait()
    loads[5].wait()

    def sweep_planes(n, base, offsets, faces, part=range(R // GROUP)):
        field = press[n - 1]
        makers = ghosts(n, base)
        low, high = zero_tile, zero_tile
        fresh = []
        for at_z in offsets:
            z = base + at_z
            for g in part:
                rows = pl.ds(g * GROUP, GROUP)
                v, *others = around(field, z, g, at_z, makers)
                news = []
                for h in range(2):
                    at = pl.ds(TOP + g * GROUP, GROUP)
                    flux = src[h, z, rows, :] + wz[h, z, rows, :] * field[h, z, at, :]
                    flux = flux + wz[h, z + 1, rows, :] * field[h, z + 2, at, :]
                    for ref, other in zip((wyl, wyh, wxl, wxh), others):
                        flux = flux + ref[h, z, rows, :] * other[h]
                    if n == 1:
                        acc[h, z // RATIO, rows, :] += flux - dia[h, z, rows, :] * v[h]
                    new = (1.0 - OMEGA) * v[h] + dinv[h, z, rows, :] * flux
                    if n < SWEEPS:
                        press[n][h, z + 1, at, :] = new
                        news.append(new)
                    else:
                        out[z, rows, pl.ds(h * H, H)] = new + corr[z // RATIO, h, rows, :]
                if 1 < n < SWEEPS:
                    fresh.append((news, g, at_z))
        if n in (1, SWEEPS):
            return faces
        for news, g, at_z in fresh:
            low, high = edges_of(news, g, at_z, low, high)
        place = lax.rem(lane, 16)
        if isinstance(base, int):
            mine = functools.reduce(jnp.logical_or, [place == base + at_z for at_z in offsets])
        else:
            low, high = pltpu.roll(low, base, 1), pltpu.roll(high, base, 1)
            mine = jnp.logical_and(place >= base + offsets[0], place <= base + offsets[-1])
        tile = lane // 16
        mine = jnp.logical_and(mine, tile >= part[0] * GROUP // 8)
        mine = jnp.logical_and(mine, tile < (part[-1] + 1) * GROUP // 8)
        return jnp.where(mine, low, faces[0]), jnp.where(mine, high, faces[1])

    none = (zero_tile, zero_tile)
    rim = (0, D - 1)

    def sweep(n, between=lambda: None):
        def inner(i, faces):
            return sweep_planes(n, 2 * i + 1, (0, 1), faces)

        count = D // 2 - 1
        if n == 1:
            arrive(fine_copy, n, range(2, 6))
            lax.fori_loop(0, count, inner, none)
            arrive(fine_copy, n, (0, 1, 6, 7))
            sweep_planes(n, 0, rim, none)
            return
        first, second = range(CHUNK // GROUP), range(CHUNK // GROUP, R // GROUP)
        arrive(fine_copy, n, range(6))
        faces = sweep_planes(n, 0, rim, none, first)
        if n < SWEEPS:
            faces = lax.fori_loop(0, 1, inner, faces)
            start(fine_copy, n + 1, (0, 1))
        faces = lax.fori_loop(1 if n < SWEEPS else 0, count, inner, faces)
        between()
        arrive(fine_copy, n, (6, 7))
        faces = sweep_planes(n, 0, rim, faces, second)
        if n < SWEEPS:
            keep_packed(n + 1, faces)
            start(fine_copy, n + 1, (4, 5, 2, 3, 6, 7))

    sweep(1)

    resid = select_dot(
        jnp.concatenate([halves(lambda h: tile_sum(acc[h, c])) for c in range(2)], 0), gsum[...], 0
    )
    rhs = pair(resid[:8], resid[8:])
    fixed = scale * rhs

    own_f[0] = fixed
    coarse_start(1, "x")
    start(fine_copy, 2, (2, 3, 0, 1))
    keep_packed(2, pack_field(p1))
    start(fine_copy, 2, (4, 5, 6, 7))
    push_weights()

    coarse_arrive(1, "x")
    merge(1)
    coarse_start(1, "z")
    def turn_to_y(q):
        near_z = (-1, 1)
        coarse_arrive(q, "z", near_z)
        coarse_start(q, "y", (0, 1))
        coarse_arrive(q, "z", [dz for dz in far if dz not in near_z])
        coarse_start(q, "y", (2, 3, 4, 5))

    turn_to_y(0)
    sweep(2, lambda: turn_to_y(1))

    def extended(q, b, n):
        _, _, z_q, y_q = groups[q]
        if b in (0, BLOCKS - 1):
            return jnp.concatenate([zero_tile, z_q[b, n], zero_tile], 0)
        return jnp.concatenate([y_q[0, b - 1, n], z_q[b, n], y_q[1, b - 1, n]], 0)

    def other_slot(v):
        return pltpu.roll(v, SLOT, 1)

    coarse_arrive(0, "y")
    turned = [other_slot(extended(0, b, 0)) if b else None for b in range(BLOCKS)]
    tall = 3 * RATIO
    for b in range(1, BLOCKS - 1):
        wz_b, wy_b, wx_b, scale_b = [extended(0, b, n) for n in range(4)]
        high = (
            jnp.where(even, turned[b], turned[b + 1]),
            pltpu.roll(wy_b, tall - 1, 0),
            pltpu.roll(wx_b, 127, 1),
        )
        for n, w in enumerate((wz_b, high[0], wy_b, high[1], wx_b, high[2])):
            sides[b - 1, n] = scale_b * w

    coarse_arrive(1, "y")
    start_values = [extended(1, b, 0) for b in range(BLOCKS)]
    e = list(start_values)
    for m in range(1, COARSE_SWEEPS):
        turned = [other_slot(v) for v in e]
        following = list(e)
        for b in range(1, BLOCKS - 1):
            if 2 * abs(b - REACH) - 1 > COARSE_SWEEPS - 1 - m:
                continue
            beside = (
                jnp.where(even, turned[b - 1], turned[b]),
                jnp.where(even, turned[b], turned[b + 1]),
                pltpu.roll(e[b], 1, 0),
                pltpu.roll(e[b], tall - 1, 0),
                pltpu.roll(e[b], 1, 1),
                pltpu.roll(e[b], 127, 1),
            )
            new = (1.0 - OMEGA) * e[b] + start_values[b]
            for n, g in enumerate(beside):
                new = new + sides[b - 1, n] * g
            following[b] = new
        e = following
    swept = e[REACH][RATIO : 2 * RATIO]

    def share(buf, ssem, rsem, me, peers):
        count = len(peers) + 1
        for peer in peers:
            pltpu.make_async_remote_copy(
                src_ref=buf.at[me], dst_ref=buf.at[me], send_sem=ssem.at[0], recv_sem=rsem.at[0],
                device_id=peer, device_id_type=MESH,
            ).start()

        others = pltpu.make_async_remote_copy(
            src_ref=buf.at[pl.ds(0, count - 1)], dst_ref=buf.at[pl.ds(0, count - 1)],
            send_sem=ssem.at[0], recv_sem=rsem.at[0],
            device_id=peers[0], device_id_type=MESH,
        )

        def finish():
            others.wait_recv()
            return jnp.sum(buf[...], axis=0)

        return finish, others.wait_send

    mine = jnp.sum(rhs - outside * swept, keepdims=True)
    part1[my_plane] = jnp.where(lane == 0, mine, jnp.where(lane == 1, diag_sum, 0.0))
    finish1, drain1 = share(part1, a1send, a1recv, my_plane, plane_peers)

    both = jnp.concatenate([swept, pltpu.roll(swept, SLOT, 1)], 0)
    spread = select_dot(both, gsum[...], 1)
    for c in range(2):
        for h in range(2):
            values = spread[8 * c : 8 * c + 8, h * H : h * H + H]
            corr[c, h] = jnp.broadcast_to(values[:, None, :], (T, RATIO, H)).reshape(R, H)

    sweep(3)
    part2[ix] = finish1()
    finish2, drain2 = share(part2, a2send, a2recv, ix, line_peers)

    sweep(SWEEPS)

    for f in range(5):
        for d in range(8):
            @pl.when(dirs[d % 6][2])
            def _():
                fine_copy(f, d).wait_send()
    for q in range(2):
        for stage in ("x", "z", "y"):
            coarse_sent(q, stage)
    drain1()

    sums = finish2()
    drain2()
    top = jnp.sum(jnp.where(lane == 0, sums, 0.0), keepdims=True)
    bottom = jnp.sum(jnp.where(lane == 1, sums, 0.0), keepdims=True)
    shift = top / bottom

    @pl.loop(0, D // 4)
    def _(i):
        for j in range(4):
            out[4 * i + j] = out[4 * i + j] + shift


def solution(mesh):
    nx, ny, nz = mesh.shape["gx"], mesh.shape["gy"], mesh.shape["gz"]
    f32, bf16 = jnp.float32, jnp.bfloat16
    dma = pltpu.SemaphoreType.DMA

    def body(*refs):
        kernel(nx, ny, nz, *refs)

    def shards(*arrays):
        block = pltpu.VMEM((2, D, R, H), f32)
        ghosted = pltpu.VMEM((2, D + 2, R + 2 * TOP, H), f32)
        return pl.pallas_call(
            body,
            out_shape=jax.ShapeDtypeStruct((D, R, W), f32),
            in_specs=[pl.BlockSpec(memory_space=pltpu.HBM)] * 3,
            out_specs=pl.BlockSpec(memory_space=pltpu.VMEM),
            scratch_shapes=[
                ghosted, ghosted, ghosted, ghosted, ghosted,
                block, pltpu.VMEM((2, D + 1, R, H), f32), block, block, block, block, block, block,
                pltpu.VMEM((2, 2, R, H), f32),
                pltpu.VMEM((W, 128), bf16), pltpu.VMEM((W, 128), bf16),
                pltpu.VMEM((2, 2, R, H), f32),
                pltpu.VMEM((5, 2, 8, 128), f32), pltpu.VMEM((5, 2, 8, 128), f32),
                *[
                    pltpu.VMEM(lead + (count, 8, 128), f32)
                    for count in (4, 1)
                    for lead in ((), (2,), (BLOCKS,), (2, BLOCKS - 2))
                ],
                pltpu.VMEM((BLOCKS - 2, 6, 3 * RATIO, 128), f32),
                pltpu.VMEM((ny * nz, 1, 128), f32), pltpu.VMEM((nx, 1, 128), f32),
                dma((3, 2)), dma((5, 8)), dma((5, 8)),
                dma((2, 2)), dma((2, 2)), dma((2, BLOCKS)), dma((2, BLOCKS)), dma((2, 6)), dma((2, 6)),
                dma((1,)), dma((1,)), dma((1,)), dma((1,)),
            ],
            compiler_params=pltpu.CompilerParams(
                collective_id=0, has_side_effects=True, vmem_limit_bytes=40 << 20
            ),
        )(*[pltpu.with_memory_space_constraint(a, pltpu.HBM) for a in arrays])

    spec = P("gx", "gy", "gz")
    return jax.shard_map(
        shards, mesh=mesh, in_specs=(spec, spec, spec), out_specs=spec, check_vma=False
    )
```

```python
import functools

import jax
import jax.numpy as jnp
from jax import lax
from jax.experimental import pallas as pl
from jax.experimental.pallas import tpu as pltpu
from jax.sharding import PartitionSpec as P

RATIO = 8
SWEEPS = 4
COARSE_SWEEPS = 8
OMEGA = 0.8
MESH = pl.DeviceIdType.MESH

D, R, W = 16, 64, 256
T = R // RATIO
H = W // 2
TOP = 8
SLOT = 64
FIRST = 8
CX = W // RATIO
REACH = 4
BLOCKS = 2 * REACH + 1
KF = 0
CHUNK = R // 2
GROUP = 16


def iota(shape, axis):
    return lax.broadcasted_iota(jnp.int32, shape, axis)


def split3(a):
    high = a.astype(jnp.bfloat16)
    rest = a - high.astype(jnp.float32)
    mid = rest.astype(jnp.bfloat16)
    low = (rest - mid.astype(jnp.float32)).astype(jnp.bfloat16)
    return jnp.concatenate([high, mid, low], axis=0)


def select_dot(a, matrix, contract):
    n = a.shape[0]
    b = lax.dot_general(
        split3(a), matrix, (((1,), (contract,)), ((), ())), preferred_element_type=jnp.float32
    )
    return b[:n] + b[n : 2 * n] + b[2 * n :]


def kernel(
    nx, ny, nz,
    p_hbm, s_hbm, k_hbm, out,
    kx, p0, p1, p2, p3, src, wz, wyl, wyh, wxl, wxh, dia, dinv, acc, gsum, gpick, corr,
    xsend, xrecv, own_w, xw, zw, yw, own_f, xf, zf, yf, sides, part1, part2,
    load_sem, fsend, frecv, cxs, cxr, czs, czr, cys, cyr, a1send, a1recv, a2send, a2recv,
):
    ix, iy, iz = lax.axis_index("gx"), lax.axis_index("gy"), lax.axis_index("gz")
    dirs = (
        ("gx", ix - 1, ix > 0), ("gx", ix + 1, ix < nx - 1),
        ("gy", iy - 1, iy > 0), ("gy", iy + 1, iy < ny - 1),
        ("gz", iz - 1, iz > 0), ("gz", iz + 1, iz < nz - 1),
    )
    press = (p0, p1, p2, p3)
    plane_group = ny * nz
    my_plane = iy * nz + iz
    own = pl.ds(TOP, R)
    planes = pl.ds(1, D)

    loads = []
    for n, (ref, place) in enumerate(((k_hbm, kx), (p_hbm, p0), (s_hbm, src))):
        for h in range(2):
            there = place.at[h, planes, own] if n < 2 else place.at[h]
            loads.append(
                pltpu.make_async_copy(ref.at[:, :, pl.ds(h * H, H)], there, load_sem.at[n])
            )
    for load in loads:
        load.start()

    def loaded(n):
        pltpu.make_async_copy((k_hbm, p_hbm, s_hbm)[n], out, load_sem.at[n]).wait()

    barrier = pltpu.get_barrier_semaphore()

    plane_peers = [
        {"gy": lax.rem(iy + dy, ny), "gz": lax.rem(iz + dz, nz)}
        for dy in range(ny) for dz in range(nz) if dy or dz
    ]
    line_peers = [{"gx": lax.rem(ix + step, nx)} for step in range(1, nx)]

    for axis, other, exists in dirs:
        @pl.when(exists)
        def _():
            pl.semaphore_signal(barrier, 1, device_id={axis: other}, device_id_type=MESH)

    for peer in plane_peers + line_peers:
        pl.semaphore_signal(barrier, 1, device_id=peer, device_id_type=MESH)

    near = sum(e.astype(jnp.int32) for _, _, e in dirs)
    lane = iota((1, 128), 1)
    zero_tile = jnp.zeros((8, 128), jnp.float32)
    edge_row = (TOP, TOP + R - 1)
    ghost_row = (TOP - 1, TOP + R)

    for d, (_, _, exists) in enumerate(dirs):
        @pl.when(jnp.logical_not(exists))
        def _():
            for f in range(1, 5):
                if d < 2:
                    press[f - 1][:, d * (D + 1), own] = jnp.zeros((2, R, H), jnp.float32)
                elif d < 4:
                    row = pl.ds(ghost_row[d - 2], 1)
                    press[f - 1][:, planes, row] = jnp.zeros((2, D, 1, H), jnp.float32)
                else:
                    xrecv[f, d - 4] = zero_tile
            if d >= 4:
                for place in (xw, xf):
                    place[d - 4] = jnp.zeros(place.shape[1:], jnp.float32)
            elif d >= 2:
                for place in (yw, yf):
                    place[d - 2] = jnp.zeros(place.shape[1:], jnp.float32)
    far = {}
    for dz in range(-REACH, REACH + 1):
        if dz:
            far[dz] = jnp.logical_and(ix + dz >= 0, ix + dz < nx)

            @pl.when(jnp.logical_not(far[dz]))
            def _():
                for place in (zw, zf):
                    place[dz + REACH] = jnp.zeros(place.shape[1:], jnp.float32)

    acc[...] = jnp.zeros(acc.shape, jnp.float32)

    def fine_copy(f, d, incoming=False):
        chunk, d = d // 6, d % 6
        axis, other, _ = dirs[d]
        rows = pl.ds(TOP + chunk * CHUNK, CHUNK)
        shift = 6 * chunk
        end = d ^ 1
        field = kx if f == KF else press[f - 1]
        if d < 2:
            here = field.at[:, 1 if d == 0 else D, rows]
            there = field.at[:, D + 1 if d == 0 else 0, rows]
            back = field.at[:, 0 if d == 0 else D + 1, rows]
        elif d < 4:
            here = field.at[:, planes, pl.ds(edge_row[d - 2], 1)]
            there = field.at[:, planes, pl.ds(ghost_row[end - 2], 1)]
            back = field.at[:, planes, pl.ds(ghost_row[d - 2], 1)]
        else:
            here, there, back = xsend.at[f, d - 4], xrecv.at[f, end - 4], xrecv.at[f, d - 4]
        return pltpu.make_async_remote_copy(
            src_ref=here,
            dst_ref=back if incoming else there,
            send_sem=fsend.at[f % 2, d + shift],
            recv_sem=frecv.at[f % 3, (d if incoming else end) + shift],
            device_id={axis: other},
            device_id_type=MESH,
        )

    groups = ((own_w, xw, zw, yw), (own_f, xf, zf, yf))

    def coarse_copy(q, stage, way, incoming=False):
        own_q, x_q, z_q, y_q = groups[q]
        if stage == "z":
            slot = REACH + way if incoming else REACH - way
            here, there = z_q.at[REACH], z_q.at[slot]
            if q == 0 and abs(way) == REACH:
                here, there = here.at[pl.ds(0, 1)], there.at[pl.ds(0, 1)]
            sems, to = (czs, czr), {"gx": ix + way}
            sent = REACH + way
            sent, slot = sent - (sent > REACH), slot - (slot > REACH)
            first_sem = 2 * REACH * q
        else:
            piece, side = way // 2, way % 2
            axis, other, _ = dirs[(4 if stage == "x" else 2) + side]
            slot = way if incoming else way ^ 1
            if stage == "x":
                here, there, sems = own_q, x_q.at[slot], (cxs, cxr)
            else:
                pieces = ((REACH - 2, 3), (0, REACH - 2), (REACH + 1, REACH - 2))
                first, size = pieces[piece] if q == 0 else (0, BLOCKS - 2)
                here = z_q.at[pl.ds(first + 1, size)]
                there = y_q.at[slot % 2, pl.ds(first, size)]
                sems = (cys, cyr)
            to, sent = {axis: other}, way
            first_sem = (2 if stage == "x" else 6) * q
        return pltpu.make_async_remote_copy(
            src_ref=here, dst_ref=there, send_sem=sems[0].at[first_sem + sent],
            recv_sem=sems[1].at[first_sem + slot], device_id=to, device_id_type=MESH,
        )

    def ways(q, stage, incoming):
        if stage == "z":
            useless = (-REACH if incoming else REACH) if q == 0 else 0
            return [(way, exists) for way, exists in far.items() if way != useless]
        first = 4 if stage == "x" else 2
        return [(way, dirs[first + way % 2][2]) for way in range(6 if stage == "y" and q == 0 else 2)]

    def coarse_start(q, stage, only=None):
        for way, exists in ways(q, stage, False):
            if only is not None and way not in only:
                continue

            @pl.when(exists)
            def _():
                coarse_copy(q, stage, way).start()

    def coarse_arrive(q, stage, only=None):
        for way, exists in ways(q, stage, True):
            if only is not None and way not in only:
                continue

            @pl.when(exists)
            def _():
                coarse_copy(q, stage, way, True).wait_recv()

    def coarse_sent(q, stage):
        for way, exists in ways(q, stage, False):
            @pl.when(exists)
            def _():
                coarse_copy(q, stage, way).wait_send()

    def start(make, f, which):
        for d in which:
            @pl.when(dirs[d % 6][2])
            def _():
                if f >= 2:
                    make(f - 2, d).wait_send()
                make(f, d).start()

    def arrive(make, f, which):
        for d in which:
            @pl.when(dirs[d % 6][2])
            def _():
                make(f, d, True).wait_recv()

    def edges_of(news, g, at_z, low, high):
        n = GROUP // 8
        for t in range(g * n, g * n + n):
            to = 16 * t + at_z
            part = slice(8 * (t - g * n), 8 * (t - g * n) + 8)
            left, right = news[0][part], news[1][part]
            low = jnp.where(lane == to, pltpu.roll(left, to, 1) if to else left, low)
            high = jnp.where(
                lane == to, pltpu.roll(right, to + 1, 1) if to < 127 else right, high
            )
        return low, high

    def keep_packed(f, faces):
        xsend[f, 0] = faces[0]
        xsend[f, 1] = faces[1]

    def ghosts(f, base):
        back = lax.rem(128 - base, 128) if not isinstance(base, int) else (128 - base) % 128
        low, high = xrecv[f, 0], xrecv[f, 1]
        if not isinstance(base, int) or base:
            low, high = pltpu.roll(low, back, 1), pltpu.roll(high, back, 1)

        def turn(v, by):
            return pltpu.roll(v, by % 128, 1) if by % 128 else v

        return (
            lambda at, t: turn(low, 128 - 16 * t - at),
            lambda at, t: turn(high, 255 - 16 * t - at),
        )

    def around(field, z, g, at_z, makers):
        n = GROUP // 8
        lows, highs = [
            jnp.concatenate([make(at_z, t) for t in range(g * n, g * n + n)], 0) for make in makers
        ]
        at = TOP + g * GROUP
        own_rows = [field[h, z + 1, pl.ds(at, GROUP), :] for h in range(2)]
        low_y = [field[h, z + 1, pl.ds(at - 1, GROUP), :] for h in range(2)]
        high_y = [field[h, z + 1, pl.ds(at + 1, GROUP), :] for h in range(2)]
        rl, rr = [pltpu.roll(v, 1, 1) for v in own_rows]
        low_x = [jnp.where(lane == 0, lows, rl), jnp.where(lane == 0, rl, rr)]
        sl, sr = [pltpu.roll(v, H - 1, 1) for v in own_rows]
        high_x = [jnp.where(lane == H - 1, sr, sl), jnp.where(lane == H - 1, highs, sr)]
        return own_rows, low_y, high_y, low_x, high_x

    def pack_field(field):
        def pack(i, faces):
            z = 4 * i
            fresh = (zero_tile, zero_tile)
            for j in range(4):
                for g in range(R // GROUP):
                    at = pl.ds(TOP + g * GROUP, GROUP)
                    rows = [field[h, z + 1 + j, at, :] for h in range(2)]
                    fresh = edges_of(rows, g, j, *fresh)
            mine = lax.rem(lane, 16) // 4 == i
            return tuple(jnp.where(mine, pltpu.roll(a, z, 1), b) for a, b in zip(fresh, faces))

        return lax.fori_loop(0, D // 4, pack, (zero_tile, zero_tile), unroll=2)

    loaded(0)
    keep_packed(KF, pack_field(kx))
    pl.semaphore_wait(barrier, near + (plane_group - 1) + (nx - 1))
    start(fine_copy, KF, (4, 5, 2, 3, 0, 1, 6, 7))
    loaded(1)
    keep_packed(1, pack_field(p0))
    start(fine_copy, 1, (4, 5, 2, 3, 0, 1, 6, 7))

    for d, (_, _, exists) in enumerate(dirs):
        @pl.when(jnp.logical_not(exists))
        def _():
            if d < 2:
                kx[:, d * (D + 1), own] = kx[:, 1 + d * (D - 1), own]
            elif d < 4:
                kx[:, planes, pl.ds(ghost_row[d - 2], 1)] = kx[:, planes, pl.ds(edge_row[d - 2], 1)]
            else:
                xrecv[KF, d - 4] = xsend[KF, d - 4]

    column, spot = iota((W, 128), 0), iota((W, 128), 1)
    home = spot == FIRST + column // RATIO
    gsum[...] = jnp.where(home, 1.0, 0.0).astype(jnp.bfloat16)
    gpick[...] = jnp.where(
        jnp.logical_and(home, lax.rem(column, RATIO) == 0), 1.0, 0.0
    ).astype(jnp.bfloat16)

    arrive(fine_copy, KF, range(2, 6))

    def weigh(base, offsets):
        makers = ghosts(KF, base)
        for at_z in offsets:
            z = base + at_z
            for g in range(R // GROUP):
                rows = pl.ds(g * GROUP, GROUP)
                k, *others = around(kx, z, g, at_z, makers)
                for h in range(2):
                    at = pl.ds(TOP + g * GROUP, GROUP)
                    half = 0.5 * k[h]
                    low_z = half + 0.5 * kx[h, z, at, :]
                    high_z = half + 0.5 * kx[h, z + 2, at, :]
                    total = low_z + high_z
                    wz[h, z, rows, :] = low_z
                    for ref, other in zip((wyl, wyh, wxl, wxh), others):
                        face = half + 0.5 * other[h]
                        ref[h, z, rows, :] = face
                        total = total + face
                    dia[h, z, rows, :] = total
                    dinv[h, z, rows, :] = OMEGA / total

    @pl.loop(0, D // 2 - 1)
    def _(i):
        weigh(2 * i + 1, (0, 1))

    arrive(fine_copy, KF, (0, 1, 6, 7))
    weigh(0, (0, D - 1))
    for h in range(2):
        wz[h, D] = 0.5 * (kx[h, D, own, :] + kx[h, D + 1, own, :])

    def tile_sum(plane):
        return jnp.sum(plane.reshape(T, RATIO, H), axis=1)

    def wide(parts):
        return jnp.concatenate(parts, axis=1)

    def halves(make):
        return wide([make(0), make(1)])

    def sum_planes(c, load):
        total = load(RATIO * c)
        for z in range(RATIO * c + 1, RATIO * c + RATIO):
            total = total + load(z)
        return total

    def every(ref, h, c, first):
        return sum_planes(c, lambda z: ref[h, z, pl.ds(first, T, stride=RATIO), :])

    summed, picked, last = [], [], []
    for c in range(2):
        summed += [
            halves(lambda h: tile_sum(wz[h, RATIO * c])),
            halves(lambda h: tile_sum(wz[h, RATIO * c + RATIO])),
            halves(lambda h: every(wyl, h, c, 0)),
            halves(lambda h: every(wyh, h, c, RATIO - 1)),
        ]
        picked.append(halves(lambda h: tile_sum(sum_planes(c, lambda z: wxl[h, z]))))
        last.append(tile_sum(sum_planes(c, lambda z: wxh[1, z])))
    sums = select_dot(jnp.concatenate(summed, 0), gsum[...], 0)
    picks = select_dot(jnp.concatenate(picked, 0), gpick[...], 0)

    def pair(low, high):
        return low + pltpu.roll(high, SLOT, 1)

    zl, zh, yl, yh = [pair(sums[8 * n : 8 * n + 8], sums[8 * n + 32 : 8 * n + 40]) for n in range(4)]
    xl = pair(picks[:8], picks[8:])
    inside = lax.rem(lane, SLOT)
    final_lane = FIRST + CX - 1
    xh = pltpu.roll(xl, 127, 1)
    for c in range(2):
        to = c * SLOT + final_lane
        xh = jnp.where(lane == to, pltpu.roll(last[c], (to + 1) % 128, 1), xh)
    valid = jnp.logical_and(inside >= FIRST, inside <= final_lane)
    xh = jnp.where(valid, xh, 0.0)
    cdiag = zl + zh + yl + yh + xl + xh
    scale = jnp.where(valid, OMEGA / jnp.where(valid, cdiag, 1.0), 0.0)
    weights = (zl, zh, yl, yh, xl, xh)
    for n, field in enumerate((zl, yl, xl, scale)):
        own_w[n] = field
    coarse_start(0, "x")
    tile_row = iota((8, 1), 0)
    even = lane < SLOT
    edges = (
        even, jnp.logical_not(even), tile_row == 0, tile_row == 7,
        inside == FIRST, inside == final_lane,
    )
    outside = zero_tile
    for (_, _, exists), edge, w in zip(dirs, edges, weights):
        gone = jnp.where(exists, 0.0, 1.0)
        outside = outside + jnp.where(edge, gone * w, 0.0)
    diag_sum = jnp.sum(cdiag, keepdims=True)

    def merge(q):
        own_q, x_q, z_q, _ = groups[q]
        for n in range(own_q.shape[0]):
            low, high = pltpu.roll(x_q[0, n], 128 - CX, 1), pltpu.roll(x_q[1, n], CX, 1)
            after = jnp.logical_and(inside > final_lane, inside <= final_lane + RATIO)
            z_q[REACH, n] = jnp.where(inside < FIRST, low, jnp.where(after, high, own_q[n]))

    def push_weights():
        coarse_arrive(0, "x")
        merge(0)
        coarse_start(0, "z")

    loaded(2)

    def sweep_planes(n, base, offsets, faces, part=range(R // GROUP)):
        field = press[n - 1]
        makers = ghosts(n, base)
        low, high = zero_tile, zero_tile
        fresh = []
        for at_z in offsets:
            z = base + at_z
            for g in part:
                rows = pl.ds(g * GROUP, GROUP)
                v, *others = around(field, z, g, at_z, makers)
                news = []
                for h in range(2):
                    at = pl.ds(TOP + g * GROUP, GROUP)
                    flux = src[h, z, rows, :] + wz[h, z, rows, :] * field[h, z, at, :]
                    flux = flux + wz[h, z + 1, rows, :] * field[h, z + 2, at, :]
                    for ref, other in zip((wyl, wyh, wxl, wxh), others):
                        flux = flux + ref[h, z, rows, :] * other[h]
                    if n == 1:
                        acc[h, z // RATIO, rows, :] += flux - dia[h, z, rows, :] * v[h]
                    new = (1.0 - OMEGA) * v[h] + dinv[h, z, rows, :] * flux
                    if n < SWEEPS:
                        press[n][h, z + 1, at, :] = new
                        news.append(new)
                    else:
                        out[z, rows, pl.ds(h * H, H)] = new + corr[z // RATIO, h, rows, :]
                if 1 < n < SWEEPS:
                    fresh.append((news, g, at_z))
        if n in (1, SWEEPS):
            return faces
        for news, g, at_z in fresh:
            low, high = edges_of(news, g, at_z, low, high)
        place = lax.rem(lane, 16)
        if isinstance(base, int):
            mine = functools.reduce(jnp.logical_or, [place == base + at_z for at_z in offsets])
        else:
            low, high = pltpu.roll(low, base, 1), pltpu.roll(high, base, 1)
            mine = jnp.logical_and(place >= base + offsets[0], place <= base + offsets[-1])
        tile = lane // 16
        mine = jnp.logical_and(mine, tile >= part[0] * GROUP // 8)
        mine = jnp.logical_and(mine, tile < (part[-1] + 1) * GROUP // 8)
        return jnp.where(mine, low, faces[0]), jnp.where(mine, high, faces[1])

    none = (zero_tile, zero_tile)
    rim = (0, D - 1)

    def sweep(n, between=lambda: None):
        def inner(i, faces):
            return sweep_planes(n, 2 * i + 1, (0, 1), faces)

        count = D // 2 - 1
        if n == 1:
            arrive(fine_copy, n, range(2, 6))
            lax.fori_loop(0, count, inner, none)
            arrive(fine_copy, n, (0, 1, 6, 7))
            sweep_planes(n, 0, rim, none)
            return
        first, second = range(CHUNK // GROUP), range(CHUNK // GROUP, R // GROUP)
        arrive(fine_copy, n, range(6))
        faces = sweep_planes(n, 0, rim, none, first)
        if n < SWEEPS:
            faces = lax.fori_loop(0, 1, inner, faces)
            start(fine_copy, n + 1, (0, 1))
        faces = lax.fori_loop(1 if n < SWEEPS else 0, count, inner, faces)
        between()
        arrive(fine_copy, n, (6, 7))
        faces = sweep_planes(n, 0, rim, faces, second)
        if n < SWEEPS:
            keep_packed(n + 1, faces)
            start(fine_copy, n + 1, (4, 5, 2, 3, 6, 7))

    sweep(1)

    resid = select_dot(
        jnp.concatenate([halves(lambda h: tile_sum(acc[h, c])) for c in range(2)], 0), gsum[...], 0
    )
    rhs = pair(resid[:8], resid[8:])
    fixed = scale * rhs

    own_f[0] = fixed
    coarse_start(1, "x")
    start(fine_copy, 2, (2, 3, 0, 1))
    keep_packed(2, pack_field(p1))
    start(fine_copy, 2, (4, 5, 6, 7))
    push_weights()

    coarse_arrive(1, "x")
    merge(1)
    coarse_start(1, "z")
    def turn_to_y(q):
        near_z = (-1, 1)
        coarse_arrive(q, "z", near_z)
        if q == 0:
            coarse_start(q, "y", (0, 1))
        coarse_arrive(q, "z", [dz for dz in far if dz not in near_z])
        coarse_start(q, "y", (2, 3, 4, 5) if q == 0 else (0, 1))

    turn_to_y(0)
    sweep(2, lambda: turn_to_y(1))

    def extended(q, b, n):
        _, _, z_q, y_q = groups[q]
        if b in (0, BLOCKS - 1):
            return jnp.concatenate([zero_tile, z_q[b, n], zero_tile], 0)
        return jnp.concatenate([y_q[0, b - 1, n], z_q[b, n], y_q[1, b - 1, n]], 0)

    def other_slot(v):
        return pltpu.roll(v, SLOT, 1)

    coarse_arrive(0, "y")
    turned = [other_slot(extended(0, b, 0)) if b else None for b in range(BLOCKS)]
    tall = 3 * RATIO
    for b in range(1, BLOCKS - 1):
        wz_b, wy_b, wx_b, scale_b = [extended(0, b, n) for n in range(4)]
        high = (
            jnp.where(even, turned[b], turned[b + 1]),
            pltpu.roll(wy_b, tall - 1, 0),
            pltpu.roll(wx_b, 127, 1),
        )
        for n, w in enumerate((wz_b, high[0], wy_b, high[1], wx_b, high[2])):
            sides[b - 1, n] = scale_b * w

    coarse_arrive(1, "y")
    start_values = [extended(1, b, 0) for b in range(BLOCKS)]
    e = list(start_values)
    for m in range(1, COARSE_SWEEPS):
        turned = [other_slot(v) for v in e]
        following = list(e)
        for b in range(1, BLOCKS - 1):
            if 2 * abs(b - REACH) - 1 > COARSE_SWEEPS - 1 - m:
                continue
            beside = (
                jnp.where(even, turned[b - 1], turned[b]),
                jnp.where(even, turned[b], turned[b + 1]),
                pltpu.roll(e[b], 1, 0),
                pltpu.roll(e[b], tall - 1, 0),
                pltpu.roll(e[b], 1, 1),
                pltpu.roll(e[b], 127, 1),
            )
            new = (1.0 - OMEGA) * e[b] + start_values[b]
            for n, g in enumerate(beside):
                new = new + sides[b - 1, n] * g
            following[b] = new
        e = following
    swept = e[REACH][RATIO : 2 * RATIO]

    def share(buf, ssem, rsem, me, peers):
        count = len(peers) + 1
        for peer in peers:
            pltpu.make_async_remote_copy(
                src_ref=buf.at[me], dst_ref=buf.at[me], send_sem=ssem.at[0], recv_sem=rsem.at[0],
                device_id=peer, device_id_type=MESH,
            ).start()

        others = pltpu.make_async_remote_copy(
            src_ref=buf.at[pl.ds(0, count - 1)], dst_ref=buf.at[pl.ds(0, count - 1)],
            send_sem=ssem.at[0], recv_sem=rsem.at[0],
            device_id=peers[0], device_id_type=MESH,
        )

        def finish():
            others.wait_recv()
            return jnp.sum(buf[...], axis=0)

        return finish, others.wait_send

    mine = jnp.sum(rhs - outside * swept, keepdims=True)
    part1[my_plane] = jnp.where(lane == 0, mine, jnp.where(lane == 1, diag_sum, 0.0))
    finish1, drain1 = share(part1, a1send, a1recv, my_plane, plane_peers)

    both = jnp.concatenate([swept, pltpu.roll(swept, SLOT, 1)], 0)
    spread = select_dot(both, gsum[...], 1)
    for c in range(2):
        for h in range(2):
            values = spread[8 * c : 8 * c + 8, h * H : h * H + H]
            corr[c, h] = jnp.broadcast_to(values[:, None, :], (T, RATIO, H)).reshape(R, H)

    sweep(3)
    part2[ix] = finish1()
    finish2, drain2 = share(part2, a2send, a2recv, ix, line_peers)

    sweep(SWEEPS)

    for f in (3, 4):
        for d in range(8):
            @pl.when(dirs[d % 6][2])
            def _():
                fine_copy(f, d).wait_send()
    for q in range(2):
        for stage in ("x", "z", "y"):
            coarse_sent(q, stage)
    drain1()

    sums = finish2()
    drain2()
    top = jnp.sum(jnp.where(lane == 0, sums, 0.0), keepdims=True)
    bottom = jnp.sum(jnp.where(lane == 1, sums, 0.0), keepdims=True)
    shift = top / bottom

    @pl.loop(0, D // 4)
    def _(i):
        for j in range(4):
            out[4 * i + j] = out[4 * i + j] + shift


def solution(mesh):
    nx, ny, nz = mesh.shape["gx"], mesh.shape["gy"], mesh.shape["gz"]
    f32, bf16 = jnp.float32, jnp.bfloat16
    dma = pltpu.SemaphoreType.DMA

    def body(*refs):
        kernel(nx, ny, nz, *refs)

    def shards(*arrays):
        block = pltpu.VMEM((2, D, R, H), f32)
        ghosted = pltpu.VMEM((2, D + 2, R + 2 * TOP, H), f32)
        return pl.pallas_call(
            body,
            out_shape=jax.ShapeDtypeStruct((D, R, W), f32),
            in_specs=[pl.BlockSpec(memory_space=pltpu.HBM)] * 3,
            out_specs=pl.BlockSpec(memory_space=pltpu.VMEM),
            scratch_shapes=[
                ghosted, ghosted, ghosted, ghosted, ghosted,
                block, pltpu.VMEM((2, D + 1, R, H), f32), block, block, block, block, block, block,
                pltpu.VMEM((2, 2, R, H), f32),
                pltpu.VMEM((W, 128), bf16), pltpu.VMEM((W, 128), bf16),
                pltpu.VMEM((2, 2, R, H), f32),
                pltpu.VMEM((5, 2, 8, 128), f32), pltpu.VMEM((5, 2, 8, 128), f32),
                *[
                    pltpu.VMEM(lead + (count, 8, 128), f32)
                    for count in (4, 1)
                    for lead in ((), (2,), (BLOCKS,), (2, BLOCKS - 2))
                ],
                pltpu.VMEM((BLOCKS - 2, 6, 3 * RATIO, 128), f32),
                pltpu.VMEM((ny * nz, 1, 128), f32), pltpu.VMEM((nx, 1, 128), f32),
                dma((3,)), dma((2, 8)), dma((3, 8)),
                dma((4,)), dma((4,)), dma((4 * REACH,)), dma((4 * REACH,)), dma((8,)), dma((8,)),
                dma((1,)), dma((1,)), dma((1,)), dma((1,)),
            ],
            compiler_params=pltpu.CompilerParams(
                collective_id=0, has_side_effects=True, vmem_limit_bytes=40 << 20
            ),
        )(*[pltpu.with_memory_space_constraint(a, pltpu.HBM) for a in arrays])

    spec = P("gx", "gy", "gz")
    return jax.shard_map(
        shards, mesh=mesh, in_specs=(spec, spec, spec), out_specs=spec, check_vma=False
    )
```

```python
import functools

import jax
import jax.numpy as jnp
from jax import lax
from jax.experimental import pallas as pl
from jax.experimental.pallas import tpu as pltpu
from jax.sharding import PartitionSpec as P

RATIO = 8
SWEEPS = 4
COARSE_SWEEPS = 8
OMEGA = 0.8
MESH = pl.DeviceIdType.MESH

D, R, W = 16, 64, 256
T = R // RATIO
H = W // 2
TOP = 8
SLOT = 64
FIRST = 8
CX = W // RATIO
REACH = 4
BLOCKS = 2 * REACH + 1
KF = 0
PAUSE = 4
CHUNK = R // 2
GROUP = 16


def iota(shape, axis):
    return lax.broadcasted_iota(jnp.int32, shape, axis)


def split3(a):
    high = a.astype(jnp.bfloat16)
    rest = a - high.astype(jnp.float32)
    mid = rest.astype(jnp.bfloat16)
    low = (rest - mid.astype(jnp.float32)).astype(jnp.bfloat16)
    return jnp.concatenate([high, mid, low], axis=0)


def select_dot(a, matrix, contract):
    n = a.shape[0]
    b = lax.dot_general(
        split3(a), matrix, (((1,), (contract,)), ((), ())), preferred_element_type=jnp.float32
    )
    return b[:n] + b[n : 2 * n] + b[2 * n :]


def kernel(
    nx, ny, nz,
    p_hbm, s_hbm, k_hbm, out,
    kx, p0, p1, p2, p3, src, wz, wyl, wyh, wxl, wxh, dia, dinv, acc, gsum, gpick, corr,
    xsend, xrecv, own_w, xw, zw, yw, own_f, xf, zf, yf, sides, part1, part2,
    load_sem, fsend, frecv, cxs, cxr, czs, czr, cys, cyr, a1send, a1recv, a2send, a2recv,
):
    ix, iy, iz = lax.axis_index("gx"), lax.axis_index("gy"), lax.axis_index("gz")
    dirs = (
        ("gx", ix - 1, ix > 0), ("gx", ix + 1, ix < nx - 1),
        ("gy", iy - 1, iy > 0), ("gy", iy + 1, iy < ny - 1),
        ("gz", iz - 1, iz > 0), ("gz", iz + 1, iz < nz - 1),
    )
    press = (p0, p1, p2, p3)
    plane_group = ny * nz
    my_plane = iy * nz + iz
    own = pl.ds(TOP, R)
    planes = pl.ds(1, D)

    loads = []
    for n, (ref, place) in enumerate(((k_hbm, kx), (p_hbm, p0), (s_hbm, src))):
        for h in range(2):
            there = place.at[h, planes, own] if n < 2 else place.at[h]
            loads.append(
                pltpu.make_async_copy(ref.at[:, :, pl.ds(h * H, H)], there, load_sem.at[n])
            )
    for load in loads:
        load.start()

    def loaded(n):
        pltpu.make_async_copy((k_hbm, p_hbm, s_hbm)[n], out, load_sem.at[n]).wait()

    barrier = pltpu.get_barrier_semaphore()

    plane_peers = [
        {"gy": lax.rem(iy + dy, ny), "gz": lax.rem(iz + dz, nz)}
        for dy in range(ny) for dz in range(nz) if dy or dz
    ]
    line_peers = [{"gx": lax.rem(ix + step, nx)} for step in range(1, nx)]

    for axis, other, exists in dirs:
        @pl.when(exists)
        def _():
            pl.semaphore_signal(barrier, 1, device_id={axis: other}, device_id_type=MESH)

    for peer in plane_peers + line_peers:
        pl.semaphore_signal(barrier, 1, device_id=peer, device_id_type=MESH)

    near = sum(e.astype(jnp.int32) for _, _, e in dirs)
    lane = iota((1, 128), 1)
    zero_tile = jnp.zeros((8, 128), jnp.float32)
    edge_row = (TOP, TOP + R - 1)
    ghost_row = (TOP - 1, TOP + R)

    for d, (_, _, exists) in enumerate(dirs):
        @pl.when(jnp.logical_not(exists))
        def _():
            for f in range(1, 5):
                if d < 2:
                    press[f - 1][:, d * (D + 1), own] = jnp.zeros((2, R, H), jnp.float32)
                elif d < 4:
                    row = pl.ds(ghost_row[d - 2], 1)
                    press[f - 1][:, planes, row] = jnp.zeros((2, D, 1, H), jnp.float32)
                else:
                    xrecv[f, d - 4] = zero_tile
            if d >= 4:
                for place in (xw, xf):
                    place[d - 4] = jnp.zeros(place.shape[1:], jnp.float32)
            elif d >= 2:
                for place in (yw, yf):
                    place[d - 2] = jnp.zeros(place.shape[1:], jnp.float32)
    far = {}
    for dz in range(-REACH, REACH + 1):
        if dz:
            far[dz] = jnp.logical_and(ix + dz >= 0, ix + dz < nx)

            @pl.when(jnp.logical_not(far[dz]))
            def _():
                for place in (zw, zf):
                    place[dz + REACH] = jnp.zeros(place.shape[1:], jnp.float32)

    acc[...] = jnp.zeros(acc.shape, jnp.float32)

    def fine_copy(f, d, incoming=False):
        chunk, d = d // 6, d % 6
        axis, other, _ = dirs[d]
        rows = pl.ds(TOP + chunk * CHUNK, CHUNK)
        shift = 6 * chunk
        end = d ^ 1
        field = kx if f == KF else press[f - 1]
        if d < 2:
            here = field.at[:, 1 if d == 0 else D, rows]
            there = field.at[:, D + 1 if d == 0 else 0, rows]
            back = field.at[:, 0 if d == 0 else D + 1, rows]
        elif d < 4:
            here = field.at[:, planes, pl.ds(edge_row[d - 2], 1)]
            there = field.at[:, planes, pl.ds(ghost_row[end - 2], 1)]
            back = field.at[:, planes, pl.ds(ghost_row[d - 2], 1)]
        else:
            here, there, back = xsend.at[f, d - 4], xrecv.at[f, end - 4], xrecv.at[f, d - 4]
        return pltpu.make_async_remote_copy(
            src_ref=here,
            dst_ref=back if incoming else there,
            send_sem=fsend.at[f % 2, d + shift],
            recv_sem=frecv.at[f % 3, (d if incoming else end) + shift],
            device_id={axis: other},
            device_id_type=MESH,
        )

    groups = ((own_w, xw, zw, yw), (own_f, xf, zf, yf))

    def coarse_copy(q, stage, way, incoming=False):
        own_q, x_q, z_q, y_q = groups[q]
        if stage == "z":
            slot = REACH + way if incoming else REACH - way
            here, there = z_q.at[REACH], z_q.at[slot]
            if q == 0 and abs(way) == REACH:
                here, there = here.at[pl.ds(0, 1)], there.at[pl.ds(0, 1)]
            sems, to = (czs, czr), {"gx": ix + way}
            sent = REACH + way
            sent, slot = sent - (sent > REACH), slot - (slot > REACH)
            first_sem = 2 * REACH * q
        else:
            piece, side = way // 2, way % 2
            axis, other, _ = dirs[(4 if stage == "x" else 2) + side]
            slot = way if incoming else way ^ 1
            if stage == "x":
                here, there, sems = own_q, x_q.at[slot], (cxs, cxr)
            else:
                pieces = ((REACH - 2, 3), (0, REACH - 2), (REACH + 1, REACH - 2))
                first, size = pieces[piece] if q == 0 else (0, BLOCKS - 2)
                here = z_q.at[pl.ds(first + 1, size)]
                there = y_q.at[slot % 2, pl.ds(first, size)]
                sems = (cys, cyr)
            to, sent = {axis: other}, way
            first_sem = (2 if stage == "x" else 6) * q
        return pltpu.make_async_remote_copy(
            src_ref=here, dst_ref=there, send_sem=sems[0].at[first_sem + sent],
            recv_sem=sems[1].at[first_sem + slot], device_id=to, device_id_type=MESH,
        )

    def ways(q, stage, incoming):
        if stage == "z":
            useless = (-REACH if incoming else REACH) if q == 0 else 0
            return [(way, exists) for way, exists in far.items() if way != useless]
        first = 4 if stage == "x" else 2
        return [(way, dirs[first + way % 2][2]) for way in range(6 if stage == "y" and q == 0 else 2)]

    def coarse_start(q, stage, only=None):
        for way, exists in ways(q, stage, False):
            if only is not None and way not in only:
                continue

            @pl.when(exists)
            def _():
                coarse_copy(q, stage, way).start()

    def coarse_arrive(q, stage, only=None):
        for way, exists in ways(q, stage, True):
            if only is not None and way not in only:
                continue

            @pl.when(exists)
            def _():
                coarse_copy(q, stage, way, True).wait_recv()

    def coarse_sent(q, stage):
        for way, exists in ways(q, stage, False):
            @pl.when(exists)
            def _():
                coarse_copy(q, stage, way).wait_send()

    def start(make, f, which):
        for d in which:
            @pl.when(dirs[d % 6][2])
            def _():
                if f >= 2:
                    make(f - 2, d).wait_send()
                make(f, d).start()

    def arrive(make, f, which):
        for d in which:
            @pl.when(dirs[d % 6][2])
            def _():
                make(f, d, True).wait_recv()

    def edges_of(news, g, at_z, low, high):
        n = GROUP // 8
        for t in range(g * n, g * n + n):
            to = 16 * t + at_z
            part = slice(8 * (t - g * n), 8 * (t - g * n) + 8)
            left, right = news[0][part], news[1][part]
            low = jnp.where(lane == to, pltpu.roll(left, to, 1) if to else left, low)
            high = jnp.where(
                lane == to, pltpu.roll(right, to + 1, 1) if to < 127 else right, high
            )
        return low, high

    def keep_packed(f, faces):
        xsend[f, 0] = faces[0]
        xsend[f, 1] = faces[1]

    def ghosts(f, base):
        back = lax.rem(128 - base, 128) if not isinstance(base, int) else (128 - base) % 128
        low, high = xrecv[f, 0], xrecv[f, 1]
        if not isinstance(base, int) or base:
            low, high = pltpu.roll(low, back, 1), pltpu.roll(high, back, 1)

        def turn(v, by):
            return pltpu.roll(v, by % 128, 1) if by % 128 else v

        return (
            lambda at, t: turn(low, 128 - 16 * t - at),
            lambda at, t: turn(high, 255 - 16 * t - at),
        )

    def around(field, z, g, at_z, makers):
        n = GROUP // 8
        lows, highs = [
            jnp.concatenate([make(at_z, t) for t in range(g * n, g * n + n)], 0) for make in makers
        ]
        at = TOP + g * GROUP
        own_rows = [field[h, z + 1, pl.ds(at, GROUP), :] for h in range(2)]
        low_y = [field[h, z + 1, pl.ds(at - 1, GROUP), :] for h in range(2)]
        high_y = [field[h, z + 1, pl.ds(at + 1, GROUP), :] for h in range(2)]
        rl, rr = [pltpu.roll(v, 1, 1) for v in own_rows]
        low_x = [jnp.where(lane == 0, lows, rl), jnp.where(lane == 0, rl, rr)]
        sl, sr = [pltpu.roll(v, H - 1, 1) for v in own_rows]
        high_x = [jnp.where(lane == H - 1, sr, sl), jnp.where(lane == H - 1, highs, sr)]
        return own_rows, low_y, high_y, low_x, high_x

    def pack_field(field):
        def pack(i, faces):
            z = 4 * i
            fresh = (zero_tile, zero_tile)
            for j in range(4):
                for g in range(R // GROUP):
                    at = pl.ds(TOP + g * GROUP, GROUP)
                    rows = [field[h, z + 1 + j, at, :] for h in range(2)]
                    fresh = edges_of(rows, g, j, *fresh)
            mine = lax.rem(lane, 16) // 4 == i
            return tuple(jnp.where(mine, pltpu.roll(a, z, 1), b) for a, b in zip(fresh, faces))

        return lax.fori_loop(0, D // 4, pack, (zero_tile, zero_tile), unroll=2)

    loaded(0)
    keep_packed(KF, pack_field(kx))
    pl.semaphore_wait(barrier, near + (plane_group - 1) + (nx - 1))
    start(fine_copy, KF, (4, 5, 2, 3, 0, 1, 6, 7))
    loaded(1)
    keep_packed(1, pack_field(p0))
    start(fine_copy, 1, (4, 5, 2, 3, 0, 1, 6, 7))

    for d, (_, _, exists) in enumerate(dirs):
        @pl.when(jnp.logical_not(exists))
        def _():
            if d < 2:
                kx[:, d * (D + 1), own] = kx[:, 1 + d * (D - 1), own]
            elif d < 4:
                kx[:, planes, pl.ds(ghost_row[d - 2], 1)] = kx[:, planes, pl.ds(edge_row[d - 2], 1)]
            else:
                xrecv[KF, d - 4] = xsend[KF, d - 4]

    column, spot = iota((W, 128), 0), iota((W, 128), 1)
    home = spot == FIRST + column // RATIO
    gsum[...] = jnp.where(home, 1.0, 0.0).astype(jnp.bfloat16)
    gpick[...] = jnp.where(
        jnp.logical_and(home, lax.rem(column, RATIO) == 0), 1.0, 0.0
    ).astype(jnp.bfloat16)

    arrive(fine_copy, KF, range(2, 6))

    def weigh(base, offsets):
        makers = ghosts(KF, base)
        for at_z in offsets:
            z = base + at_z
            for g in range(R // GROUP):
                rows = pl.ds(g * GROUP, GROUP)
                k, *others = around(kx, z, g, at_z, makers)
                for h in range(2):
                    at = pl.ds(TOP + g * GROUP, GROUP)
                    half = 0.5 * k[h]
                    low_z = half + 0.5 * kx[h, z, at, :]
                    high_z = half + 0.5 * kx[h, z + 2, at, :]
                    total = low_z + high_z
                    wz[h, z, rows, :] = low_z
                    for ref, other in zip((wyl, wyh, wxl, wxh), others):
                        face = half + 0.5 * other[h]
                        ref[h, z, rows, :] = face
                        total = total + face
                    dia[h, z, rows, :] = total
                    dinv[h, z, rows, :] = OMEGA / total

    @pl.loop(0, D // 2 - 1)
    def _(i):
        weigh(2 * i + 1, (0, 1))

    arrive(fine_copy, KF, (0, 1, 6, 7))
    weigh(0, (0, D - 1))
    for h in range(2):
        wz[h, D] = 0.5 * (kx[h, D, own, :] + kx[h, D + 1, own, :])

    def tile_sum(plane):
        return jnp.sum(plane.reshape(T, RATIO, H), axis=1)

    def wide(parts):
        return jnp.concatenate(parts, axis=1)

    def halves(make):
        return wide([make(0), make(1)])

    def sum_planes(c, load):
        total = load(RATIO * c)
        for z in range(RATIO * c + 1, RATIO * c + RATIO):
            total = total + load(z)
        return total

    def every(ref, h, c, first):
        return sum_planes(c, lambda z: ref[h, z, pl.ds(first, T, stride=RATIO), :])

    summed, picked, last = [], [], []
    for c in range(2):
        summed += [
            halves(lambda h: tile_sum(wz[h, RATIO * c])),
            halves(lambda h: tile_sum(wz[h, RATIO * c + RATIO])),
            halves(lambda h: every(wyl, h, c, 0)),
            halves(lambda h: every(wyh, h, c, RATIO - 1)),
        ]
        picked.append(halves(lambda h: tile_sum(sum_planes(c, lambda z: wxl[h, z]))))
        last.append(tile_sum(sum_planes(c, lambda z: wxh[1, z])))
    sums = select_dot(jnp.concatenate(summed, 0), gsum[...], 0)
    picks = select_dot(jnp.concatenate(picked, 0), gpick[...], 0)

    def pair(low, high):
        return low + pltpu.roll(high, SLOT, 1)

    zl, zh, yl, yh = [pair(sums[8 * n : 8 * n + 8], sums[8 * n + 32 : 8 * n + 40]) for n in range(4)]
    xl = pair(picks[:8], picks[8:])
    inside = lax.rem(lane, SLOT)
    final_lane = FIRST + CX - 1
    xh = pltpu.roll(xl, 127, 1)
    for c in range(2):
        to = c * SLOT + final_lane
        xh = jnp.where(lane == to, pltpu.roll(last[c], (to + 1) % 128, 1), xh)
    valid = jnp.logical_and(inside >= FIRST, inside <= final_lane)
    xh = jnp.where(valid, xh, 0.0)
    cdiag = zl + zh + yl + yh + xl + xh
    scale = jnp.where(valid, OMEGA / jnp.where(valid, cdiag, 1.0), 0.0)
    weights = (zl, zh, yl, yh, xl, xh)
    for n, field in enumerate((zl, yl, xl, scale)):
        own_w[n] = field
    coarse_start(0, "x")
    tile_row = iota((8, 1), 0)
    even = lane < SLOT
    edges = (
        even, jnp.logical_not(even), tile_row == 0, tile_row == 7,
        inside == FIRST, inside == final_lane,
    )
    outside = zero_tile
    for (_, _, exists), edge, w in zip(dirs, edges, weights):
        gone = jnp.where(exists, 0.0, 1.0)
        outside = outside + jnp.where(edge, gone * w, 0.0)
    diag_sum = jnp.sum(cdiag, keepdims=True)

    def merge(q):
        own_q, x_q, z_q, _ = groups[q]
        for n in range(own_q.shape[0]):
            low, high = pltpu.roll(x_q[0, n], 128 - CX, 1), pltpu.roll(x_q[1, n], CX, 1)
            after = jnp.logical_and(inside > final_lane, inside <= final_lane + RATIO)
            z_q[REACH, n] = jnp.where(inside < FIRST, low, jnp.where(after, high, own_q[n]))

    def push_weights():
        coarse_arrive(0, "x")
        merge(0)
        coarse_start(0, "z")

    loaded(2)

    def sweep_planes(n, base, offsets, faces, part=range(R // GROUP)):
        field = press[n - 1]
        makers = ghosts(n, base)
        low, high = zero_tile, zero_tile
        fresh = []
        for at_z in offsets:
            z = base + at_z
            for g in part:
                rows = pl.ds(g * GROUP, GROUP)
                v, *others = around(field, z, g, at_z, makers)
                news = []
                for h in range(2):
                    at = pl.ds(TOP + g * GROUP, GROUP)
                    flux = src[h, z, rows, :] + wz[h, z, rows, :] * field[h, z, at, :]
                    flux = flux + wz[h, z + 1, rows, :] * field[h, z + 2, at, :]
                    for ref, other in zip((wyl, wyh, wxl, wxh), others):
                        flux = flux + ref[h, z, rows, :] * other[h]
                    if n == 1:
                        acc[h, z // RATIO, rows, :] += flux - dia[h, z, rows, :] * v[h]
                    new = (1.0 - OMEGA) * v[h] + dinv[h, z, rows, :] * flux
                    if n < SWEEPS:
                        press[n][h, z + 1, at, :] = new
                        news.append(new)
                    else:
                        out[z, rows, pl.ds(h * H, H)] = new + corr[z // RATIO, h, rows, :]
                if 1 < n < SWEEPS:
                    fresh.append((news, g, at_z))
        if n in (1, SWEEPS):
            return faces
        for news, g, at_z in fresh:
            low, high = edges_of(news, g, at_z, low, high)
        place = lax.rem(lane, 16)
        if isinstance(base, int):
            mine = functools.reduce(jnp.logical_or, [place == base + at_z for at_z in offsets])
        else:
            low, high = pltpu.roll(low, base, 1), pltpu.roll(high, base, 1)
            mine = jnp.logical_and(place >= base + offsets[0], place <= base + offsets[-1])
        tile = lane // 16
        mine = jnp.logical_and(mine, tile >= part[0] * GROUP // 8)
        mine = jnp.logical_and(mine, tile < (part[-1] + 1) * GROUP // 8)
        return jnp.where(mine, low, faces[0]), jnp.where(mine, high, faces[1])

    none = (zero_tile, zero_tile)
    rim = (0, D - 1)

    def sweep(n, between=None):
        def inner(i, faces):
            return sweep_planes(n, 2 * i + 1, (0, 1), faces)

        count = D // 2 - 1
        if n == 1:
            arrive(fine_copy, n, range(2, 6))
            lax.fori_loop(0, count, inner, none)
            arrive(fine_copy, n, (0, 1, 6, 7))
            sweep_planes(n, 0, rim, none)
            return
        first, second = range(CHUNK // GROUP), range(CHUNK // GROUP, R // GROUP)
        arrive(fine_copy, n, range(6))
        faces = sweep_planes(n, 0, rim, none, first)
        if n < SWEEPS:
            faces = lax.fori_loop(0, 1, inner, faces)
            start(fine_copy, n + 1, (0, 1))
        middle = 1 if n < SWEEPS else 0
        if between is not None:
            faces = lax.fori_loop(middle, PAUSE, inner, faces)
            between()
            middle = PAUSE
        faces = lax.fori_loop(middle, count, inner, faces)
        arrive(fine_copy, n, (6, 7))
        faces = sweep_planes(n, 0, rim, faces, second)
        if n < SWEEPS:
            keep_packed(n + 1, faces)
            start(fine_copy, n + 1, (4, 5, 2, 3, 6, 7))

    sweep(1)

    resid = select_dot(
        jnp.concatenate([halves(lambda h: tile_sum(acc[h, c])) for c in range(2)], 0), gsum[...], 0
    )
    rhs = pair(resid[:8], resid[8:])
    fixed = scale * rhs

    own_f[0] = fixed
    coarse_start(1, "x")
    keep_packed(2, pack_field(p1))
    start(fine_copy, 2, (4, 5, 2, 3, 0, 1, 6, 7))
    push_weights()

    coarse_arrive(1, "x")
    merge(1)
    coarse_start(1, "z")
    def turn_to_y(q):
        near_z = (-1, 1)
        coarse_arrive(q, "z", near_z)
        if q == 0:
            coarse_start(q, "y", (0, 1))
        coarse_arrive(q, "z", [dz for dz in far if dz not in near_z])
        coarse_start(q, "y", (2, 3, 4, 5) if q == 0 else (0, 1))

    turn_to_y(0)
    sweep(2, lambda: turn_to_y(1))

    def extended(q, b, n):
        _, _, z_q, y_q = groups[q]
        if b in (0, BLOCKS - 1):
            return jnp.concatenate([zero_tile, z_q[b, n], zero_tile], 0)
        return jnp.concatenate([y_q[0, b - 1, n], z_q[b, n], y_q[1, b - 1, n]], 0)

    def other_slot(v):
        return pltpu.roll(v, SLOT, 1)

    coarse_arrive(0, "y")
    turned = [other_slot(extended(0, b, 0)) if b else None for b in range(BLOCKS)]
    tall = 3 * RATIO
    for b in range(1, BLOCKS - 1):
        wz_b, wy_b, wx_b, scale_b = [extended(0, b, n) for n in range(4)]
        high = (
            jnp.where(even, turned[b], turned[b + 1]),
            pltpu.roll(wy_b, tall - 1, 0),
            pltpu.roll(wx_b, 127, 1),
        )
        for n, w in enumerate((wz_b, high[0], wy_b, high[1], wx_b, high[2])):
            sides[b - 1, n] = scale_b * w

    coarse_arrive(1, "y")
    start_values = [extended(1, b, 0) for b in range(BLOCKS)]
    e = list(start_values)
    for m in range(1, COARSE_SWEEPS):
        turned = [other_slot(v) for v in e]
        following = list(e)
        for b in range(1, BLOCKS - 1):
            if 2 * abs(b - REACH) - 1 > COARSE_SWEEPS - 1 - m:
                continue
            beside = (
                jnp.where(even, turned[b - 1], turned[b]),
                jnp.where(even, turned[b], turned[b + 1]),
                pltpu.roll(e[b], 1, 0),
                pltpu.roll(e[b], tall - 1, 0),
                pltpu.roll(e[b], 1, 1),
                pltpu.roll(e[b], 127, 1),
            )
            new = (1.0 - OMEGA) * e[b] + start_values[b]
            for n, g in enumerate(beside):
                new = new + sides[b - 1, n] * g
            following[b] = new
        e = following
    swept = e[REACH][RATIO : 2 * RATIO]

    def share(buf, ssem, rsem, me, peers):
        count = len(peers) + 1
        for peer in peers:
            pltpu.make_async_remote_copy(
                src_ref=buf.at[me], dst_ref=buf.at[me], send_sem=ssem.at[0], recv_sem=rsem.at[0],
                device_id=peer, device_id_type=MESH,
            ).start()

        others = pltpu.make_async_remote_copy(
            src_ref=buf.at[pl.ds(0, count - 1)], dst_ref=buf.at[pl.ds(0, count - 1)],
            send_sem=ssem.at[0], recv_sem=rsem.at[0],
            device_id=peers[0], device_id_type=MESH,
        )

        def finish():
            others.wait_recv()
            return jnp.sum(buf[...], axis=0)

        return finish, others.wait_send

    mine = jnp.sum(rhs - outside * swept, keepdims=True)
    part1[my_plane] = jnp.where(lane == 0, mine, jnp.where(lane == 1, diag_sum, 0.0))
    finish1, drain1 = share(part1, a1send, a1recv, my_plane, plane_peers)

    both = jnp.concatenate([swept, pltpu.roll(swept, SLOT, 1)], 0)
    spread = select_dot(both, gsum[...], 1)
    for c in range(2):
        for h in range(2):
            values = spread[8 * c : 8 * c + 8, h * H : h * H + H]
            corr[c, h] = jnp.broadcast_to(values[:, None, :], (T, RATIO, H)).reshape(R, H)

    sweep(3)
    part2[ix] = finish1()
    finish2, drain2 = share(part2, a2send, a2recv, ix, line_peers)

    sweep(SWEEPS)

    for f in (3, 4):
        for d in range(8):
            @pl.when(dirs[d % 6][2])
            def _():
                fine_copy(f, d).wait_send()
    for q in range(2):
        for stage in ("x", "z", "y"):
            coarse_sent(q, stage)
    drain1()

    sums = finish2()
    drain2()
    top = jnp.sum(jnp.where(lane == 0, sums, 0.0), keepdims=True)
    bottom = jnp.sum(jnp.where(lane == 1, sums, 0.0), keepdims=True)
    shift = top / bottom

    @pl.loop(0, D // 4)
    def _(i):
        for j in range(4):
            out[4 * i + j] = out[4 * i + j] + shift


def solution(mesh):
    nx, ny, nz = mesh.shape["gx"], mesh.shape["gy"], mesh.shape["gz"]
    f32, bf16 = jnp.float32, jnp.bfloat16
    dma = pltpu.SemaphoreType.DMA

    def body(*refs):
        kernel(nx, ny, nz, *refs)

    def shards(*arrays):
        block = pltpu.VMEM((2, D, R, H), f32)
        ghosted = pltpu.VMEM((2, D + 2, R + 2 * TOP, H), f32)
        return pl.pallas_call(
            body,
            out_shape=jax.ShapeDtypeStruct((D, R, W), f32),
            in_specs=[pl.BlockSpec(memory_space=pltpu.HBM)] * 3,
            out_specs=pl.BlockSpec(memory_space=pltpu.VMEM),
            scratch_shapes=[
                ghosted, ghosted, ghosted, ghosted, ghosted,
                block, pltpu.VMEM((2, D + 1, R, H), f32), block, block, block, block, block, block,
                pltpu.VMEM((2, 2, R, H), f32),
                pltpu.VMEM((W, 128), bf16), pltpu.VMEM((W, 128), bf16),
                pltpu.VMEM((2, 2, R, H), f32),
                pltpu.VMEM((5, 2, 8, 128), f32), pltpu.VMEM((5, 2, 8, 128), f32),
                *[
                    pltpu.VMEM(lead + (count, 8, 128), f32)
                    for count in (4, 1)
                    for lead in ((), (2,), (BLOCKS,), (2, BLOCKS - 2))
                ],
                pltpu.VMEM((BLOCKS - 2, 6, 3 * RATIO, 128), f32),
                pltpu.VMEM((ny * nz, 1, 128), f32), pltpu.VMEM((nx, 1, 128), f32),
                dma((3,)), dma((2, 8)), dma((3, 8)),
                dma((4,)), dma((4,)), dma((4 * REACH,)), dma((4 * REACH,)), dma((8,)), dma((8,)),
                dma((1,)), dma((1,)), dma((1,)), dma((1,)),
            ],
            compiler_params=pltpu.CompilerParams(
                collective_id=0, has_side_effects=True, vmem_limit_bytes=40 << 20
            ),
        )(*[pltpu.with_memory_space_constraint(a, pltpu.HBM) for a in arrays])

    spec = P("gx", "gy", "gz")
    return jax.shard_map(
        shards, mesh=mesh, in_specs=(spec, spec, spec), out_specs=spec, check_vma=False
    )
```

```python
import functools

import jax
import jax.numpy as jnp
from jax import lax
from jax.experimental import pallas as pl
from jax.experimental.pallas import tpu as pltpu
from jax.sharding import PartitionSpec as P

RATIO = 8
SWEEPS = 4
COARSE_SWEEPS = 8
OMEGA = 0.8
MESH = pl.DeviceIdType.MESH

D, R, W = 16, 64, 256
T = R // RATIO
H = W // 2
TOP = 8
SLOT = 64
FIRST = 8
CX = W // RATIO
REACH = 4
BLOCKS = 2 * REACH + 1
KF = 0
PAUSE = 4
CHUNK = R // 2
GROUP = 16


def iota(shape, axis):
    return lax.broadcasted_iota(jnp.int32, shape, axis)


def split3(a):
    high = a.astype(jnp.bfloat16)
    rest = a - high.astype(jnp.float32)
    mid = rest.astype(jnp.bfloat16)
    low = (rest - mid.astype(jnp.float32)).astype(jnp.bfloat16)
    return jnp.concatenate([high, mid, low], axis=0)


def select_dot(a, matrix, contract):
    n = a.shape[0]
    b = lax.dot_general(
        split3(a), matrix, (((1,), (contract,)), ((), ())), preferred_element_type=jnp.float32
    )
    return b[:n] + b[n : 2 * n] + b[2 * n :]


def kernel(
    nx, ny, nz,
    p_hbm, s_hbm, k_hbm, out,
    kx, p0, p1, p2, p3, src, wz, wyl, wyh, wxl, wxh, dia, dinv, acc, gsum, gpick, corr,
    xsend, xrecv, own_w, xw, zw, yw, own_f, xf, zf, yf, sides, part1, part2,
    load_sem, fsend, frecv, cxs, cxr, czs, czr, cys, cyr, a1send, a1recv, a2send, a2recv,
):
    ix, iy, iz = lax.axis_index("gx"), lax.axis_index("gy"), lax.axis_index("gz")
    dirs = (
        ("gx", ix - 1, ix > 0), ("gx", ix + 1, ix < nx - 1),
        ("gy", iy - 1, iy > 0), ("gy", iy + 1, iy < ny - 1),
        ("gz", iz - 1, iz > 0), ("gz", iz + 1, iz < nz - 1),
    )
    press = (p0, p1, p2, p3)
    plane_group = ny * nz
    my_plane = iy * nz + iz
    own = pl.ds(TOP, R)
    planes = pl.ds(1, D)

    loads = []
    for n, (ref, place) in enumerate(((k_hbm, kx), (p_hbm, p0), (s_hbm, src))):
        for h in range(2):
            there = place.at[h, planes, own] if n < 2 else place.at[h]
            loads.append(
                pltpu.make_async_copy(ref.at[:, :, pl.ds(h * H, H)], there, load_sem.at[n])
            )
    for load in loads:
        load.start()

    def loaded(n):
        pltpu.make_async_copy((k_hbm, p_hbm, s_hbm)[n], out, load_sem.at[n]).wait()

    barrier = pltpu.get_barrier_semaphore()

    plane_peers = [
        {"gy": lax.rem(iy + dy, ny), "gz": lax.rem(iz + dz, nz)}
        for dy in range(ny) for dz in range(nz) if dy or dz
    ]
    line_peers = [{"gx": lax.rem(ix + step, nx)} for step in range(1, nx)]

    for axis, other, exists in dirs:
        @pl.when(exists)
        def _():
            pl.semaphore_signal(barrier, 1, device_id={axis: other}, device_id_type=MESH)

    for peer in plane_peers + line_peers:
        pl.semaphore_signal(barrier, 1, device_id=peer, device_id_type=MESH)

    near = sum(e.astype(jnp.int32) for _, _, e in dirs)
    lane = iota((1, 128), 1)
    zero_tile = jnp.zeros((8, 128), jnp.float32)
    edge_row = (TOP, TOP + R - 1)
    ghost_row = (TOP - 1, TOP + R)

    for d, (_, _, exists) in enumerate(dirs):
        @pl.when(jnp.logical_not(exists))
        def _():
            for f in range(1, 5):
                if d < 2:
                    press[f - 1][:, d * (D + 1), own] = jnp.zeros((2, R, H), jnp.float32)
                elif d < 4:
                    row = pl.ds(ghost_row[d - 2], 1)
                    press[f - 1][:, planes, row] = jnp.zeros((2, D, 1, H), jnp.float32)
                else:
                    xrecv[f, d - 4] = zero_tile
            if d >= 4:
                for place in (xw, xf):
                    place[d - 4] = jnp.zeros(place.shape[1:], jnp.float32)
            elif d >= 2:
                for place in (yw, yf):
                    place[d - 2] = jnp.zeros(place.shape[1:], jnp.float32)
    far = {}
    for dz in range(-REACH, REACH + 1):
        if dz:
            far[dz] = jnp.logical_and(ix + dz >= 0, ix + dz < nx)

            @pl.when(jnp.logical_not(far[dz]))
            def _():
                for place in (zw, zf):
                    place[dz + REACH] = jnp.zeros(place.shape[1:], jnp.float32)

    acc[...] = jnp.zeros(acc.shape, jnp.float32)

    def fine_copy(f, d, incoming=False):
        chunk, d = d // 6, d % 6
        axis, other, _ = dirs[d]
        rows = pl.ds(TOP + chunk * CHUNK, CHUNK)
        shift = 6 * chunk
        end = d ^ 1
        field = kx if f == KF else press[f - 1]
        if d < 2:
            here = field.at[:, 1 if d == 0 else D, rows]
            there = field.at[:, D + 1 if d == 0 else 0, rows]
            back = field.at[:, 0 if d == 0 else D + 1, rows]
        elif d < 4:
            here = field.at[:, planes, pl.ds(edge_row[d - 2], 1)]
            there = field.at[:, planes, pl.ds(ghost_row[end - 2], 1)]
            back = field.at[:, planes, pl.ds(ghost_row[d - 2], 1)]
        else:
            here, there, back = xsend.at[f, d - 4], xrecv.at[f, end - 4], xrecv.at[f, d - 4]
        return pltpu.make_async_remote_copy(
            src_ref=here,
            dst_ref=back if incoming else there,
            send_sem=fsend.at[f % 2, d + shift],
            recv_sem=frecv.at[f % 3, (d if incoming else end) + shift],
            device_id={axis: other},
            device_id_type=MESH,
        )

    groups = ((own_w, xw, zw, yw), (own_f, xf, zf, yf))

    def coarse_copy(q, stage, way, incoming=False):
        own_q, x_q, z_q, y_q = groups[q]
        if stage == "z":
            slot = REACH + way if incoming else REACH - way
            here, there = z_q.at[REACH], z_q.at[slot]
            if q == 0 and abs(way) == REACH:
                here, there = here.at[pl.ds(0, 1)], there.at[pl.ds(0, 1)]
            sems, to = (czs, czr), {"gx": ix + way}
            sent = REACH + way
            sent, slot = sent - (sent > REACH), slot - (slot > REACH)
            first_sem = 2 * REACH * q
        else:
            piece, side = way // 2, way % 2
            axis, other, _ = dirs[(4 if stage == "x" else 2) + side]
            slot = way if incoming else way ^ 1
            if stage == "x":
                here, there, sems = own_q, x_q.at[slot], (cxs, cxr)
            else:
                pieces = ((REACH - 2, 3), (0, REACH - 2), (REACH + 1, REACH - 2))
                first, size = pieces[piece] if q == 0 else (0, BLOCKS - 2)
                here = z_q.at[pl.ds(first + 1, size)]
                there = y_q.at[slot % 2, pl.ds(first, size)]
                sems = (cys, cyr)
            to, sent = {axis: other}, way
            first_sem = (2 if stage == "x" else 6) * q
        return pltpu.make_async_remote_copy(
            src_ref=here, dst_ref=there, send_sem=sems[0].at[first_sem + sent],
            recv_sem=sems[1].at[first_sem + slot], device_id=to, device_id_type=MESH,
        )

    def ways(q, stage, incoming):
        if stage == "z":
            useless = (-REACH if incoming else REACH) if q == 0 else 0
            return [(way, exists) for way, exists in far.items() if way != useless]
        first = 4 if stage == "x" else 2
        return [(way, dirs[first + way % 2][2]) for way in range(6 if stage == "y" and q == 0 else 2)]

    def coarse_start(q, stage, only=None):
        for way, exists in ways(q, stage, False):
            if only is not None and way not in only:
                continue

            @pl.when(exists)
            def _():
                coarse_copy(q, stage, way).start()

    def coarse_arrive(q, stage, only=None):
        for way, exists in ways(q, stage, True):
            if only is not None and way not in only:
                continue

            @pl.when(exists)
            def _():
                coarse_copy(q, stage, way, True).wait_recv()

    def coarse_sent(q, stage):
        for way, exists in ways(q, stage, False):
            @pl.when(exists)
            def _():
                coarse_copy(q, stage, way).wait_send()

    def start(make, f, which):
        for d in which:
            @pl.when(dirs[d % 6][2])
            def _():
                if f >= 2:
                    make(f - 2, d).wait_send()
                make(f, d).start()

    def arrive(make, f, which):
        for d in which:
            @pl.when(dirs[d % 6][2])
            def _():
                make(f, d, True).wait_recv()

    def edges_of(news, g, at_z, low, high):
        n = GROUP // 8
        for t in range(g * n, g * n + n):
            to = 16 * t + at_z
            part = slice(8 * (t - g * n), 8 * (t - g * n) + 8)
            left, right = news[0][part], news[1][part]
            low = jnp.where(lane == to, pltpu.roll(left, to, 1) if to else left, low)
            high = jnp.where(
                lane == to, pltpu.roll(right, to + 1, 1) if to < 127 else right, high
            )
        return low, high

    def keep_packed(f, faces):
        xsend[f, 0] = faces[0]
        xsend[f, 1] = faces[1]

    def ghosts(f, base):
        back = lax.rem(128 - base, 128) if not isinstance(base, int) else (128 - base) % 128
        low, high = xrecv[f, 0], xrecv[f, 1]
        if not isinstance(base, int) or base:
            low, high = pltpu.roll(low, back, 1), pltpu.roll(high, back, 1)

        def turn(v, by):
            return pltpu.roll(v, by % 128, 1) if by % 128 else v

        return (
            lambda at, t: turn(low, 128 - 16 * t - at),
            lambda at, t: turn(high, 255 - 16 * t - at),
        )

    def around(field, z, g, at_z, makers):
        n = GROUP // 8
        lows, highs = [
            jnp.concatenate([make(at_z, t) for t in range(g * n, g * n + n)], 0) for make in makers
        ]
        at = TOP + g * GROUP
        own_rows = [field[h, z + 1, pl.ds(at, GROUP), :] for h in range(2)]
        low_y = [field[h, z + 1, pl.ds(at - 1, GROUP), :] for h in range(2)]
        high_y = [field[h, z + 1, pl.ds(at + 1, GROUP), :] for h in range(2)]
        rl, rr = [pltpu.roll(v, 1, 1) for v in own_rows]
        low_x = [jnp.where(lane == 0, lows, rl), jnp.where(lane == 0, rl, rr)]
        sl, sr = [pltpu.roll(v, H - 1, 1) for v in own_rows]
        high_x = [jnp.where(lane == H - 1, sr, sl), jnp.where(lane == H - 1, highs, sr)]
        return own_rows, low_y, high_y, low_x, high_x

    def pack_field(field):
        def pack(i, faces):
            z = 4 * i
            fresh = (zero_tile, zero_tile)
            for j in range(4):
                for g in range(R // GROUP):
                    at = pl.ds(TOP + g * GROUP, GROUP)
                    rows = [field[h, z + 1 + j, at, :] for h in range(2)]
                    fresh = edges_of(rows, g, j, *fresh)
            mine = lax.rem(lane, 16) // 4 == i
            return tuple(jnp.where(mine, pltpu.roll(a, z, 1), b) for a, b in zip(fresh, faces))

        return lax.fori_loop(0, D // 4, pack, (zero_tile, zero_tile), unroll=4)

    loaded(0)
    keep_packed(KF, pack_field(kx))
    pl.semaphore_wait(barrier, near + (plane_group - 1) + (nx - 1))
    start(fine_copy, KF, (4, 5, 2, 3, 0, 1, 6, 7))
    loaded(1)
    keep_packed(1, pack_field(p0))
    start(fine_copy, 1, (4, 5, 2, 3, 0, 1, 6, 7))

    for d, (_, _, exists) in enumerate(dirs):
        @pl.when(jnp.logical_not(exists))
        def _():
            if d < 2:
                kx[:, d * (D + 1), own] = kx[:, 1 + d * (D - 1), own]
            elif d < 4:
                kx[:, planes, pl.ds(ghost_row[d - 2], 1)] = kx[:, planes, pl.ds(edge_row[d - 2], 1)]
            else:
                xrecv[KF, d - 4] = xsend[KF, d - 4]

    column, spot = iota((W, 128), 0), iota((W, 128), 1)
    home = spot == FIRST + column // RATIO
    gsum[...] = jnp.where(home, 1.0, 0.0).astype(jnp.bfloat16)
    gpick[...] = jnp.where(
        jnp.logical_and(home, lax.rem(column, RATIO) == 0), 1.0, 0.0
    ).astype(jnp.bfloat16)

    arrive(fine_copy, KF, range(2, 6))

    def weigh(base, offsets):
        makers = ghosts(KF, base)
        for at_z in offsets:
            z = base + at_z
            for g in range(R // GROUP):
                rows = pl.ds(g * GROUP, GROUP)
                k, *others = around(kx, z, g, at_z, makers)
                for h in range(2):
                    at = pl.ds(TOP + g * GROUP, GROUP)
                    half = 0.5 * k[h]
                    low_z = half + 0.5 * kx[h, z, at, :]
                    high_z = half + 0.5 * kx[h, z + 2, at, :]
                    total = low_z + high_z
                    wz[h, z, rows, :] = low_z
                    for ref, other in zip((wyl, wyh, wxl, wxh), others):
                        face = half + 0.5 * other[h]
                        ref[h, z, rows, :] = face
                        total = total + face
                    dia[h, z, rows, :] = total
                    dinv[h, z, rows, :] = OMEGA / total

    @pl.loop(0, D // 2 - 1)
    def _(i):
        weigh(2 * i + 1, (0, 1))

    arrive(fine_copy, KF, (0, 1, 6, 7))
    weigh(0, (0, D - 1))
    for h in range(2):
        wz[h, D] = 0.5 * (kx[h, D, own, :] + kx[h, D + 1, own, :])

    def tile_sum(plane):
        return jnp.sum(plane.reshape(T, RATIO, H), axis=1)

    def wide(parts):
        return jnp.concatenate(parts, axis=1)

    def halves(make):
        return wide([make(0), make(1)])

    def sum_planes(c, load):
        total = load(RATIO * c)
        for z in range(RATIO * c + 1, RATIO * c + RATIO):
            total = total + load(z)
        return total

    def every(ref, h, c, first):
        return sum_planes(c, lambda z: ref[h, z, pl.ds(first, T, stride=RATIO), :])

    summed, picked, last = [], [], []
    for c in range(2):
        summed += [
            halves(lambda h: tile_sum(wz[h, RATIO * c])),
            halves(lambda h: tile_sum(wz[h, RATIO * c + RATIO])),
            halves(lambda h: every(wyl, h, c, 0)),
            halves(lambda h: every(wyh, h, c, RATIO - 1)),
        ]
        picked.append(halves(lambda h: tile_sum(sum_planes(c, lambda z: wxl[h, z]))))
        last.append(tile_sum(sum_planes(c, lambda z: wxh[1, z])))
    sums = select_dot(jnp.concatenate(summed, 0), gsum[...], 0)
    picks = select_dot(jnp.concatenate(picked, 0), gpick[...], 0)

    def pair(low, high):
        return low + pltpu.roll(high, SLOT, 1)

    zl, zh, yl, yh = [pair(sums[8 * n : 8 * n + 8], sums[8 * n + 32 : 8 * n + 40]) for n in range(4)]
    xl = pair(picks[:8], picks[8:])
    inside = lax.rem(lane, SLOT)
    final_lane = FIRST + CX - 1
    xh = pltpu.roll(xl, 127, 1)
    for c in range(2):
        to = c * SLOT + final_lane
        xh = jnp.where(lane == to, pltpu.roll(last[c], (to + 1) % 128, 1), xh)
    valid = jnp.logical_and(inside >= FIRST, inside <= final_lane)
    xh = jnp.where(valid, xh, 0.0)
    cdiag = zl + zh + yl + yh + xl + xh
    scale = jnp.where(valid, OMEGA / jnp.where(valid, cdiag, 1.0), 0.0)
    weights = (zl, zh, yl, yh, xl, xh)
    for n, field in enumerate((zl, yl, xl, scale)):
        own_w[n] = field
    coarse_start(0, "x")
    tile_row = iota((8, 1), 0)
    even = lane < SLOT
    edges = (
        even, jnp.logical_not(even), tile_row == 0, tile_row == 7,
        inside == FIRST, inside == final_lane,
    )
    outside = zero_tile
    for (_, _, exists), edge, w in zip(dirs, edges, weights):
        gone = jnp.where(exists, 0.0, 1.0)
        outside = outside + jnp.where(edge, gone * w, 0.0)
    diag_sum = jnp.sum(cdiag, keepdims=True)

    def merge(q):
        own_q, x_q, z_q, _ = groups[q]
        for n in range(own_q.shape[0]):
            low, high = pltpu.roll(x_q[0, n], 128 - CX, 1), pltpu.roll(x_q[1, n], CX, 1)
            after = jnp.logical_and(inside > final_lane, inside <= final_lane + RATIO)
            z_q[REACH, n] = jnp.where(inside < FIRST, low, jnp.where(after, high, own_q[n]))

    def push_weights():
        coarse_arrive(0, "x")
        merge(0)
        coarse_start(0, "z")

    loaded(2)

    def sweep_planes(n, base, offsets, faces, part=range(R // GROUP)):
        field = press[n - 1]
        makers = ghosts(n, base)
        low, high = zero_tile, zero_tile
        fresh = []
        for at_z in offsets:
            z = base + at_z
            for g in part:
                rows = pl.ds(g * GROUP, GROUP)
                v, *others = around(field, z, g, at_z, makers)
                news = []
                for h in range(2):
                    at = pl.ds(TOP + g * GROUP, GROUP)
                    flux = src[h, z, rows, :] + wz[h, z, rows, :] * field[h, z, at, :]
                    flux = flux + wz[h, z + 1, rows, :] * field[h, z + 2, at, :]
                    for ref, other in zip((wyl, wyh, wxl, wxh), others):
                        flux = flux + ref[h, z, rows, :] * other[h]
                    if n == 1:
                        acc[h, z // RATIO, rows, :] += flux - dia[h, z, rows, :] * v[h]
                    new = (1.0 - OMEGA) * v[h] + dinv[h, z, rows, :] * flux
                    if n < SWEEPS:
                        press[n][h, z + 1, at, :] = new
                        news.append(new)
                    else:
                        out[z, rows, pl.ds(h * H, H)] = new + corr[z // RATIO, h, rows, :]
                if 1 < n < SWEEPS:
                    fresh.append((news, g, at_z))
        if n in (1, SWEEPS):
            return faces
        for news, g, at_z in fresh:
            low, high = edges_of(news, g, at_z, low, high)
        place = lax.rem(lane, 16)
        if isinstance(base, int):
            mine = functools.reduce(jnp.logical_or, [place == base + at_z for at_z in offsets])
        else:
            low, high = pltpu.roll(low, base, 1), pltpu.roll(high, base, 1)
            mine = jnp.logical_and(place >= base + offsets[0], place <= base + offsets[-1])
        tile = lane // 16
        mine = jnp.logical_and(mine, tile >= part[0] * GROUP // 8)
        mine = jnp.logical_and(mine, tile < (part[-1] + 1) * GROUP // 8)
        return jnp.where(mine, low, faces[0]), jnp.where(mine, high, faces[1])

    none = (zero_tile, zero_tile)
    rim = (0, D - 1)

    def sweep(n, between=None):
        def inner(i, faces):
            return sweep_planes(n, 2 * i + 1, (0, 1), faces)

        count = D // 2 - 1
        if n == 1:
            arrive(fine_copy, n, range(2, 6))
            lax.fori_loop(0, count, inner, none, unroll=count)
            arrive(fine_copy, n, (0, 1, 6, 7))
            sweep_planes(n, 0, rim, none)
            return
        first, second = range(CHUNK // GROUP), range(CHUNK // GROUP, R // GROUP)
        arrive(fine_copy, n, range(6))
        faces = sweep_planes(n, 0, rim, none, first)
        if n < SWEEPS:
            faces = lax.fori_loop(0, 1, inner, faces)
            start(fine_copy, n + 1, (0, 1))
        middle = 1 if n < SWEEPS else 0
        if between is not None:
            faces = lax.fori_loop(middle, PAUSE, inner, faces)
            between()
            middle = PAUSE
        faces = lax.fori_loop(middle, count, inner, faces)
        arrive(fine_copy, n, (6, 7))
        faces = sweep_planes(n, 0, rim, faces, second)
        if n < SWEEPS:
            keep_packed(n + 1, faces)
            start(fine_copy, n + 1, (4, 5, 2, 3, 6, 7))

    sweep(1)

    resid = select_dot(
        jnp.concatenate([halves(lambda h: tile_sum(acc[h, c])) for c in range(2)], 0), gsum[...], 0
    )
    rhs = pair(resid[:8], resid[8:])
    fixed = scale * rhs

    own_f[0] = fixed
    coarse_start(1, "x")
    keep_packed(2, pack_field(p1))
    start(fine_copy, 2, (4, 5, 2, 3, 0, 1, 6, 7))
    push_weights()

    coarse_arrive(1, "x")
    merge(1)
    coarse_start(1, "z")
    def turn_to_y(q):
        near_z = (-1, 1)
        coarse_arrive(q, "z", near_z)
        if q == 0:
            coarse_start(q, "y", (0, 1))
        coarse_arrive(q, "z", [dz for dz in far if dz not in near_z])
        coarse_start(q, "y", (2, 3, 4, 5) if q == 0 else (0, 1))

    turn_to_y(0)
    sweep(2, lambda: turn_to_y(1))

    def extended(q, b, n):
        _, _, z_q, y_q = groups[q]
        if b in (0, BLOCKS - 1):
            return jnp.concatenate([zero_tile, z_q[b, n], zero_tile], 0)
        return jnp.concatenate([y_q[0, b - 1, n], z_q[b, n], y_q[1, b - 1, n]], 0)

    def other_slot(v):
        return pltpu.roll(v, SLOT, 1)

    coarse_arrive(0, "y")
    turned = [other_slot(extended(0, b, 0)) if b else None for b in range(BLOCKS)]
    tall = 3 * RATIO
    for b in range(1, BLOCKS - 1):
        wz_b, wy_b, wx_b, scale_b = [extended(0, b, n) for n in range(4)]
        high = (
            jnp.where(even, turned[b], turned[b + 1]),
            pltpu.roll(wy_b, tall - 1, 0),
            pltpu.roll(wx_b, 127, 1),
        )
        for n, w in enumerate((wz_b, high[0], wy_b, high[1], wx_b, high[2])):
            sides[b - 1, n] = scale_b * w

    coarse_arrive(1, "y")
    start_values = [extended(1, b, 0) for b in range(BLOCKS)]
    e = list(start_values)
    for m in range(1, COARSE_SWEEPS):
        turned = [other_slot(v) for v in e]
        following = list(e)
        for b in range(1, BLOCKS - 1):
            if 2 * abs(b - REACH) - 1 > COARSE_SWEEPS - 1 - m:
                continue
            beside = (
                jnp.where(even, turned[b - 1], turned[b]),
                jnp.where(even, turned[b], turned[b + 1]),
                pltpu.roll(e[b], 1, 0),
                pltpu.roll(e[b], tall - 1, 0),
                pltpu.roll(e[b], 1, 1),
                pltpu.roll(e[b], 127, 1),
            )
            new = (1.0 - OMEGA) * e[b] + start_values[b]
            for n, g in enumerate(beside):
                new = new + sides[b - 1, n] * g
            following[b] = new
        e = following
    swept = e[REACH][RATIO : 2 * RATIO]

    def share(buf, ssem, rsem, me, peers):
        count = len(peers) + 1
        for peer in peers:
            pltpu.make_async_remote_copy(
                src_ref=buf.at[me], dst_ref=buf.at[me], send_sem=ssem.at[0], recv_sem=rsem.at[0],
                device_id=peer, device_id_type=MESH,
            ).start()

        others = pltpu.make_async_remote_copy(
            src_ref=buf.at[pl.ds(0, count - 1)], dst_ref=buf.at[pl.ds(0, count - 1)],
            send_sem=ssem.at[0], recv_sem=rsem.at[0],
            device_id=peers[0], device_id_type=MESH,
        )

        def finish():
            others.wait_recv()
            return jnp.sum(buf[...], axis=0)

        return finish, others.wait_send

    mine = jnp.sum(rhs - outside * swept, keepdims=True)
    part1[my_plane] = jnp.where(lane == 0, mine, jnp.where(lane == 1, diag_sum, 0.0))
    finish1, drain1 = share(part1, a1send, a1recv, my_plane, plane_peers)

    both = jnp.concatenate([swept, pltpu.roll(swept, SLOT, 1)], 0)
    spread = select_dot(both, gsum[...], 1)
    for c in range(2):
        for h in range(2):
            values = spread[8 * c : 8 * c + 8, h * H : h * H + H]
            corr[c, h] = jnp.broadcast_to(values[:, None, :], (T, RATIO, H)).reshape(R, H)

    sweep(3)
    part2[ix] = finish1()
    finish2, drain2 = share(part2, a2send, a2recv, ix, line_peers)

    sweep(SWEEPS)

    for f in (3, 4):
        for d in range(8):
            @pl.when(dirs[d % 6][2])
            def _():
                fine_copy(f, d).wait_send()
    for q in range(2):
        for stage in ("x", "z", "y"):
            coarse_sent(q, stage)
    drain1()

    sums = finish2()
    drain2()
    top = jnp.sum(jnp.where(lane == 0, sums, 0.0), keepdims=True)
    bottom = jnp.sum(jnp.where(lane == 1, sums, 0.0), keepdims=True)
    shift = top / bottom

    @pl.loop(0, D // 4)
    def _(i):
        for j in range(4):
            out[4 * i + j] = out[4 * i + j] + shift


def solution(mesh):
    nx, ny, nz = mesh.shape["gx"], mesh.shape["gy"], mesh.shape["gz"]
    f32, bf16 = jnp.float32, jnp.bfloat16
    dma = pltpu.SemaphoreType.DMA

    def body(*refs):
        kernel(nx, ny, nz, *refs)

    def shards(*arrays):
        block = pltpu.VMEM((2, D, R, H), f32)
        ghosted = pltpu.VMEM((2, D + 2, R + 2 * TOP, H), f32)
        return pl.pallas_call(
            body,
            out_shape=jax.ShapeDtypeStruct((D, R, W), f32),
            in_specs=[pl.BlockSpec(memory_space=pltpu.HBM)] * 3,
            out_specs=pl.BlockSpec(memory_space=pltpu.VMEM),
            scratch_shapes=[
                ghosted, ghosted, ghosted, ghosted, ghosted,
                block, pltpu.VMEM((2, D + 1, R, H), f32), block, block, block, block, block, block,
                pltpu.VMEM((2, 2, R, H), f32),
                pltpu.VMEM((W, 128), bf16), pltpu.VMEM((W, 128), bf16),
                pltpu.VMEM((2, 2, R, H), f32),
                pltpu.VMEM((5, 2, 8, 128), f32), pltpu.VMEM((5, 2, 8, 128), f32),
                *[
                    pltpu.VMEM(lead + (count, 8, 128), f32)
                    for count in (4, 1)
                    for lead in ((), (2,), (BLOCKS,), (2, BLOCKS - 2))
                ],
                pltpu.VMEM((BLOCKS - 2, 6, 3 * RATIO, 128), f32),
                pltpu.VMEM((ny * nz, 1, 128), f32), pltpu.VMEM((nx, 1, 128), f32),
                dma((3,)), dma((2, 8)), dma((3, 8)),
                dma((4,)), dma((4,)), dma((4 * REACH,)), dma((4 * REACH,)), dma((8,)), dma((8,)),
                dma((1,)), dma((1,)), dma((1,)), dma((1,)),
            ],
            compiler_params=pltpu.CompilerParams(
                collective_id=0, has_side_effects=True, vmem_limit_bytes=40 << 20
            ),
        )(*[pltpu.with_memory_space_constraint(a, pltpu.HBM) for a in arrays])

    spec = P("gx", "gy", "gz")
    return jax.shard_map(
        shards, mesh=mesh, in_specs=(spec, spec, spec), out_specs=spec, check_vma=False
    )
```
